128 devices in a mesh: dir: 32 (over y, x, core), region: 4 (over z).
Axes of the slice: x: 4, y: 4, z: 4, core: 2. Of those that a mesh axis runs over, the one named last changes fastest.
Arguments:
- currents: bfloat16 [4, 192, 128, 256], P('region', 'dir'), may hold values from -6 to 6
- radiate: bfloat16 [1536, 128], replicated, may hold values from -0.5 to 0.5
- receive: bfloat16 [128, 1536], replicated, may hold values from -0.15625 to 0.15625
- transfer_table: bfloat16 [316, 1536], replicated, may hold values from -0.875 to 0.875
- near_blocks: bfloat16 [4, 192, 27, 128, 128], P('region', 'dir'), may hold values from -0.109375 to 0.109375
- dir_offsets: int32 [33], replicated, may hold values from 0 to 1536, as said below
- trans_src: int32 [4, 192, 48], P('region'), may hold values from -1 to 383, as said below
- trans_tid: int32 [4, 192, 48], P('region'), may hold values from 0 to 315
- near_src: int32 [4, 192, 27], P('region', 'dir'), may hold values from -1 to 287, as said below
Outputs:
- scattered: bfloat16 [4, 192, 128, 256], P('region', 'dir')
The draws below stay inside these ranges and needn't reach their ends.
Inputs may be any that keep to these rules, and one draw needn't show every extreme that they name: dir_offsets starts at 0, ends at 1536 and rises; every band holds 24 to 72 direction samples, and some band holds exactly 72. `trans_src`: in each box's list the non-empty slots come first and name distinct boxes; a list holds 24 to 48 of them, and some list is full. `near_src`: each box's list starts with the box itself, then names distinct other boxes, then empty slots; a list holds 13 to 27 non-empty slots, and some list is full.
All inputs are finite; a program needn't handle non-finite values.
Results may differ from the reference program's by a relative error of at most 0.005.
Values may be sent and summed in bfloat16 or wider, within the bound.
A program may use at most 192 MiB of HBM per device.

```python
import jax
import jax.numpy as jnp
from jax import lax

Q = 128
K = 1536
R = 256
NT = 316
L = 48
NN = 27
REGIONS = 4
RB = 192
HB = 96
HN = 48
N_DIR = 32


def draw_dir_offsets(key, part):
    mean_share = K // N_DIR
    half_share = mean_share // 2
    chosen = jax.random.permutation(jax.random.fold_in(key, 11), N_DIR)
    jitter = jax.random.randint(jax.random.fold_in(key, 12), (), 0, half_share)
    change = jnp.zeros((N_DIR,), jnp.int32)
    change = change.at[chosen[0]].add(half_share).at[chosen[1]].add(-half_share)
    change = change.at[chosen[2]].add(jitter).at[chosen[3]].add(-jitter)
    share_sizes = (mean_share + change).astype(jnp.int32)
    return jnp.concatenate([jnp.zeros((1,), jnp.int32), jnp.cumsum(share_sizes).astype(jnp.int32)])


def live_mask(key, rows_all, slots, least):
    live_counts = jax.random.randint(jax.random.fold_in(key, 5), (rows_all,), least, slots + 1)
    live_counts = live_counts.at[0].set(slots).at[1].set(least)
    slot_index = jnp.arange(slots, dtype=jnp.int32)
    return slot_index[None, :] < live_counts[:, None]


def draw_trans_src(key, part):
    rows_all = REGIONS * RB
    extent = RB + 2 * HB
    row_keys = jax.random.split(jax.random.fold_in(key, 21), rows_all)
    shuffled = jax.vmap(lambda row_key: jax.random.permutation(row_key, extent))(row_keys).astype(jnp.int32)
    first_top = jnp.argmax(shuffled[0] == extent - 1).astype(jnp.int32)
    shuffled = shuffled.at[0].set(jnp.roll(shuffled[0], -first_top))
    chosen = shuffled[:, :L]
    keep = live_mask(jax.random.fold_in(key, 22), rows_all, L, L // 2)
    return jnp.where(keep, chosen, -1).astype(jnp.int32).reshape(REGIONS, RB, L)


def draw_near_src(key, part):
    rows_all = REGIONS * RB
    extent = RB + 2 * HN
    row_keys = jax.random.split(jax.random.fold_in(key, 31), rows_all)
    shuffled = jax.vmap(lambda row_key: jax.random.permutation(row_key, extent - 1))(row_keys).astype(jnp.int32)
    first_top = jnp.argmax(shuffled[0] == extent - 2).astype(jnp.int32)
    shuffled = shuffled.at[0].set(jnp.roll(shuffled[0], -first_top))
    own_index = (jnp.arange(rows_all, dtype=jnp.int32) % RB + HN).astype(jnp.int32)
    others = shuffled[:, :NN - 1]
    others = others + (others >= own_index[:, None]).astype(jnp.int32)
    chosen = jnp.concatenate([own_index[:, None], others], 1)
    keep = live_mask(jax.random.fold_in(key, 32), rows_all, NN, NN // 2)
    return jnp.where(keep, chosen, -1).astype(jnp.int32).reshape(REGIONS, RB, NN)


def set_ends(drawn, rng, low, largest):
    place = [jax.random.randint(jax.random.fold_in(rng, axis), (), 0, length) for axis, length in enumerate(drawn.shape)]
    widest = drawn.shape.index(max(drawn.shape))
    beside = place[:widest] + [(place[widest] + 1) % drawn.shape[widest]] + place[widest + 1:]
    return drawn.at[tuple(place)].set(low).at[tuple(beside)].set(largest)


def block_levels(stream_key, shape, pieces, low, top_value):
    factor_of = 1.0
    for axis_at, parts in pieces:
        draws = jax.random.uniform(jax.random.fold_in(jax.random.fold_in(stream_key, 6), axis_at), (parts,), jnp.float32, low / len(pieces), top_value / len(pieces))
        factor_of = factor_of * jnp.repeat(jnp.exp(draws), shape[axis_at] // parts).reshape((-1,) + (1,) * (len(shape) - 1 - axis_at))
    return factor_of


def bell_draw(own_key, shape, width, reach, cuts=(), held_as=jnp.bfloat16):
    gain = block_levels(own_key, shape, cuts, -0.22, 0.18) if cuts else 1.0
    array = jax.random.normal(own_key, shape, jnp.float32) * width * gain
    return jnp.minimum(jnp.maximum(array, -reach), reach).astype(held_as)


def setup_inputs(seed: int = 0) -> dict:
    splits = jax.random.split(jax.random.key(seed), 10)
    currents = bell_draw(splits[0], (REGIONS, RB, Q, R), 1.0, 6.0, ((0, 4), (1, 32)))
    radiate = bell_draw(splits[1], (K, Q), Q ** -0.5, 0.5)
    receive = bell_draw(splits[2], (Q, K), K ** -0.5, 0.15625)
    transfer_table = bell_draw(splits[3], (NT, K), L ** -0.5, 0.875)
    near_blocks = bell_draw(splits[4], (REGIONS, RB, NN, Q, Q), (NN * Q) ** -0.5, 0.109375, ((0, 4), (1, 32)))
    dir_offsets = draw_dir_offsets(jax.random.fold_in(splits[9], 71), 0)
    trans_src = draw_trans_src(jax.random.fold_in(splits[9], 71), 0)
    trans_tid = set_ends(jax.random.randint(splits[7], (REGIONS, RB, L), 0, NT), jax.random.fold_in(splits[7], 1), 0, NT - 1).astype(jnp.int32)
    near_src = draw_near_src(jax.random.fold_in(splits[9], 71), 0)
    return dict(currents=currents, radiate=radiate, receive=receive, transfer_table=transfer_table, near_blocks=near_blocks, dir_offsets=dir_offsets, trans_src=trans_src, trans_tid=trans_tid, near_src=near_src)


def band_weights(offsets, directions):
    dir_count = offsets.shape[0] - 1
    position = jnp.arange(directions, dtype=jnp.int32)
    starts = offsets[:-1]
    band_ends = offsets[1:]
    inside = (position[None, :] >= starts[:, None]) & (position[None, :] < band_ends[:, None])
    per_band = directions / (dir_count * (band_ends - starts).astype(jnp.float32))
    return jnp.sum(jnp.where(inside, per_band[:, None], jnp.zeros((), jnp.float32)), axis=0)


def region_rim(blocks_all, region_index, rim_width):
    count_all = blocks_all.shape[0]
    lower_rim = lax.dynamic_index_in_dim(blocks_all, jnp.maximum(region_index - 1, 0), 0, False)[-rim_width:]
    upper_rim = lax.dynamic_index_in_dim(blocks_all, jnp.minimum(region_index + 1, count_all - 1), 0, False)[:rim_width]
    lower_rim = jnp.where(region_index > 0, lower_rim, jnp.zeros_like(lower_rim))
    upper_rim = jnp.where(region_index < count_all - 1, upper_rim, jnp.zeros_like(upper_rim))
    own_block = lax.dynamic_index_in_dim(blocks_all, region_index, 0, False)
    return jnp.concatenate([lower_rim, own_block, upper_rim], 0)


def reference(currents, radiate, receive, transfer_table, near_blocks, dir_offsets, trans_src, trans_tid, near_src):
    weights = band_weights(dir_offsets, K)
    recv_w = (receive.astype(jnp.float32) * weights[None, :]).astype(jnp.bfloat16)
    radiate_full = radiate.astype(jnp.float32)

    def aggregate(region_field):
        return jnp.einsum('kq,jqr->jkr', radiate_full, region_field.astype(jnp.float32)).astype(jnp.bfloat16)

    patterns = lax.map(aggregate, currents)

    def one_region(region_index):
        extended = region_rim(patterns, region_index, HB)
        sources = trans_src[region_index]
        classes_here = trans_tid[region_index]

        def add_entry(entry, running):
            source_col = sources[:, entry]
            class_col = classes_here[:, entry]
            gathered = jnp.take(extended, jnp.maximum(source_col, 0), axis=0).astype(jnp.float32)
            factor = jnp.take(transfer_table, class_col, axis=0).astype(jnp.float32)
            factor = jnp.where((source_col >= 0)[:, None], factor, jnp.zeros((), jnp.float32))
            return running + factor[:, :, None] * gathered

        translated = lax.fori_loop(0, L, add_entry, jnp.zeros((RB, K, R), jnp.float32)).astype(jnp.bfloat16)
        far_field = jnp.einsum('qk,jkr->jqr', recv_w.astype(jnp.float32), translated.astype(jnp.float32))
        near_ext = region_rim(currents, region_index, HN)
        near_here = near_src[region_index]
        picked = jnp.take(near_ext, jnp.maximum(near_here, 0), axis=0).astype(jnp.float32)
        picked = jnp.where((near_here >= 0)[:, :, None, None], picked, jnp.zeros((), jnp.float32))
        block_here = lax.dynamic_index_in_dim(near_blocks, region_index, 0, False).astype(jnp.float32)
        near_field = jnp.einsum('jmpq,jmqr->jpr', block_here, picked)
        return (far_field + near_field).astype(jnp.bfloat16)

    return lax.map(one_region, jnp.arange(REGIONS, dtype=jnp.int32))
```

```python
import jax
import jax.numpy as jnp
from jax import lax
from jax.experimental import pallas as pl
from jax.experimental.pallas import tpu as pltpu
from jax.sharding import PartitionSpec as P

MESH = pl.DeviceIdType.MESH
BF = jnp.bfloat16
F32 = jnp.float32
TB = 96
NCH = 6
TCH = TB // NCH


def m4(v):
    return lax.rem(v + 8, 4)


def body(
    cur_in, rad_in, rcv_in, nb_in, nsl_in, tt_t, src, tid, offs, out,
    cur, nb, mat, pat, tx, rx, relay, ps, pr, acc, buf, rad, rcv, rw, fin, nsv, ns_own, ns_par,
    lsem, psend, precv, asend, arecv, zsend, zrecv, rsend, rrecv, ssend, srecv,
):
    d = lax.axis_index("dir")
    z = lax.axis_index("region")
    c = lax.rem(d, 2)
    chip = lax.div(d, 2)
    x = lax.rem(chip, 4)
    y = lax.div(chip, 4)
    pa = x + c * (y - x)
    pb = y + c * (x - y)
    oc = 1 - c

    def dev(a, b, zz=None):
        xx = a + c * (b - a)
        yy = b + c * (a - b)
        return ((yy * 4 + xx) * 2 + c, z if zz is None else zz)

    partner = (d + 1 - 2 * c, z)
    a_up, a_dn = dev(m4(pa + 1), pb), dev(m4(pa - 1), pb)
    b_up, b_dn = dev(pa, m4(pb + 1)), dev(pa, m4(pb - 1))
    b_far = dev(pa, m4(pb + 2))
    z_up, z_dn = dev(pa, pb, m4(z + 1)), dev(pa, pb, m4(z - 1))

    barrier = pltpu.get_barrier_semaphore()
    for peer in (partner, a_up, a_dn, b_up, b_dn, b_far, z_up, z_dn):
        pl.semaphore_signal(barrier, inc=1, device_id=peer, device_id_type=MESH)
    pl.semaphore_wait(barrier, 8)

    pending = []

    def remote(src_ref, dst_ref, send, recv, to):
        return pltpu.make_async_remote_copy(
            src_ref=src_ref, dst_ref=dst_ref, send_sem=send, recv_sem=recv,
            device_id=to, device_id_type=MESH,
        )

    def go(copy):
        copy.start()
        pending.append(copy)
        return copy

    def base(oa, ob):
        return pl.multiple_of((m4(pa - oa) * 4 + m4(pb - ob)) * 16, 16)

    own0 = base(0, 0)
    give = remote(
        cur_in.at[:, :, pl.ds(pl.multiple_of(oc * 128, 128), 128)],
        cur.at[pl.ds((pb * 4 + pa) * 16 + c * 6, 6)],
        psend.at[0], precv.at[0], partner,
    )
    go(give)
    keep = pltpu.make_async_copy(
        cur_in.at[:, :, pl.ds(pl.multiple_of(c * 128, 128), 128)],
        cur.at[pl.ds(own0 + c * 6, 6)], lsem.at[0],
    )
    keep.start()
    band = pb * 4 + pa
    load_rad = pltpu.make_async_copy(
        rad_in.at[pl.ds(pl.multiple_of(band * TB, 16), TB)], rad, lsem.at[1]
    )
    load_rad.start()
    load_rcv = pltpu.make_async_copy(
        rcv_in.at[:, pl.ds(pl.multiple_of(pb * 384, 128), 384)], rcv, lsem.at[2]
    )
    load_rcv.start()
    load_ns = pltpu.make_async_copy(nsl_in.at[pl.ds(0, 8)], ns_own, lsem.at[3])
    load_ns.start()
    give_ns = remote(nsl_in.at[pl.ds(8, 8)], nsv, psend.at[1], precv.at[1], partner)
    go(give_ns)

    def arrived(ref, sem):
        remote(ref, ref, psend.at[0], sem, partner).wait_recv()

    count = [0]

    def send_main(oa, ob, lo, n, to, ra, rb, piece):
        part = cur.at[pl.ds(base(oa, ob) + lo, n)]
        go(remote(part, part, asend.at[count[0]], arecv.at[(ra * 4 + rb) * 2 + piece], to))
        count[0] += 1

    def got_main(oa, ob, lo, n, piece):
        arrived(cur.at[pl.ds(base(oa, ob) + lo, n)], arecv.at[(oa * 4 + ob) * 2 + piece])

    def z_target(oa, ob):
        a_, b_ = m4(pa - oa), m4(pb - ob)
        yb = b_ + c * (a_ - b_)
        return dev(pa, pb, m4(z + 2 * lax.div(yb, 2) - 1))

    def zb_at(oa, ob):
        a_, b_ = m4(pa - oa), m4(pb - ob)
        return 256 + ((a_ * 2 + lax.rem(b_, 2)) * 2 + lax.div(b_, 2)) * 8

    def send_zb(oa, ob):
        go(remote(
            cur.at[pl.ds(base(oa, ob) + 4, 8)], cur.at[pl.ds(zb_at(oa, ob), 8)],
            zsend.at[oa * 4 + ob], zrecv.at[oa * 4 + ob], z_target(oa, ob),
        ))

    def got_zb(oa, ob):
        arrived(cur.at[pl.ds(zb_at(oa, ob), 8)], zrecv.at[oa * 4 + ob])

    def pattern_block(at):
        def pair(i, _):
            two = jnp.concatenate([cur[at + 2 * i], cur[at + 2 * i + 1]], axis=1)
            o = jnp.dot(rad[...], two, preferred_element_type=F32)
            buf[pl.ds(pl.multiple_of(2 * i * TB, TB), TB), :] = o[:, :128]
            buf[pl.ds(pl.multiple_of(2 * i * TB + TB, TB), TB), :] = o[:, 128:]
            return 0

        lax.fori_loop(0, 8, pair, 0)

        def turn(t, _):
            pat[t, pl.ds(at, 16), :] = buf[pl.ds(t, 16, stride=TB), :].astype(BF)
            return 0

        lax.fori_loop(0, TB, turn, 0, unroll=8)

    def pattern_main(oa, ob):
        pattern_block(base(oa, ob))

    def pattern_zb(oa, ob):
        got_zb(oa, ob)
        got_zb(oa, ob + 2)
        g = m4(pa - oa) * 2 + lax.rem(m4(pb - ob), 2)
        pattern_block(pl.multiple_of(256 + g * 16, 16))

    n_iota = lax.broadcasted_iota(jnp.int32, (384, 128), 0)
    lane = lax.broadcasted_iota(jnp.int32, (TB, 128), 1)

    def hot(ref, row):
        return jnp.where(n_iota == ref[pl.ds(row, 1), :], 1.0, 0.0).astype(BF)

    def mat_group(g):
        def two_rows(it, _):
            row = g * 8 + 2 * it
            classes = jnp.concatenate([hot(tid, row), hot(tid, row + 1)], axis=1)
            coef = jnp.dot(tt_t[...], classes, preferred_element_type=F32)
            for p in range(2):
                part = coef[:, p * 128 : (p + 1) * 128]
                both = jnp.concatenate(
                    [jnp.where(lane < 64, part, 0.0), jnp.where(lane < 64, 0.0, part)], axis=0
                ).astype(BF)
                placed = lax.dot_general(
                    both, hot(src, row + p), (((1,), (1,)), ((), ())), preferred_element_type=F32
                )
                r0 = (2 * it + p) * TB
                for h in range(2):
                    for q in range(3):
                        at = pl.multiple_of(q * 1536 + h * 8 * TB + r0, 8)
                        buf[pl.ds(at, TB), :] = placed[h * TB : (h + 1) * TB, q * 128 : (q + 1) * 128]
            return 0

        lax.fori_loop(0, 4, two_rows, 0)
        j0 = pl.multiple_of(g * 16, 16)

        def turn(t, _):
            for q in range(3):
                mat[t, pl.ds(j0, 16), q * 128 : (q + 1) * 128] = buf[
                    pl.ds(q * 1536 + t, 16, stride=TB), :
                ].astype(BF)
            return 0

        lax.fori_loop(0, TB, turn, 0, unroll=4)

    def mats(lo, hi):
        lax.fori_loop(lo, hi, lambda g, _: (mat_group(g), 0)[1], 0)

    keep.wait()
    arrived(cur.at[pl.ds(own0 + oc * 6, 6)], precv.at[0])
    go(remote(
        cur.at[pl.ds(own0, 4)], cur.at[pl.ds(own0 + 12, 4)],
        zsend.at[16], zrecv.at[16], z_target(0, 0),
    ))
    send_main(0, 0, 0, 12, a_up, 1, 0, 0)
    send_main(0, 0, 0, 12, a_dn, 3, 0, 0)
    send_main(0, 0, 0, 12, b_up, 0, 1, 0)
    send_main(0, 0, 0, 12, b_dn, 0, 3, 0)
    send_zb(0, 0)
    load_nb = pltpu.make_async_copy(nb_in, nb.at[pl.ds(c * 6, 6)], lsem.at[4])
    load_nb.start()
    go(remote(nb_in, nb.at[pl.ds(c * 6, 6)], psend.at[2], precv.at[2], partner))
    cur[384] = jnp.zeros((128, 128), BF)
    arrived(cur.at[pl.ds(own0 + 12, 4)], zrecv.at[16])
    send_main(0, 0, 12, 4, a_up, 1, 0, 1)
    send_main(0, 0, 12, 4, a_dn, 3, 0, 1)
    send_main(0, 0, 12, 4, b_up, 0, 1, 1)
    send_main(0, 0, 12, 4, b_dn, 0, 3, 1)
    mats(0, 1)

    def line_event(oa):
        send_main(oa, 0, 0, 16, b_up, oa, 1, 0)
        send_main(oa, 0, 0, 16, b_dn, oa, 3, 0)
        send_zb(oa, 0)

    for oa, lo, to, piece in ((1, 0, a_up, 0), (3, 8, a_dn, 1)):
        got_main(oa, 0, 0, 12, 0)
        got_main(oa, 0, 12, 4, 1)
        send_main(oa, 0, lo, 8, to, 2, 0, piece)
        line_event(oa)
    for ob, lo, to, piece in ((1, 0, b_up, 0), (3, 8, b_dn, 1)):
        got_main(0, ob, 0, 12, 0)
        got_main(0, ob, 12, 4, 1)
        send_main(0, ob, lo, 8, to, 0, 2, piece)
        send_zb(0, ob)
    load_rad.wait()
    mats(1, 3)
    pattern_main(0, 0)
    got_main(2, 0, 0, 8, 0)
    got_main(2, 0, 8, 8, 1)
    line_event(2)
    got_main(0, 2, 0, 8, 0)
    got_main(0, 2, 8, 8, 1)
    send_zb(0, 2)
    mats(3, 4)
    pattern_main(1, 0)
    pattern_main(3, 0)
    fill = {
        (1, 3): lambda: (mats(4, 6), pattern_main(0, 1)),
        (1, 2): lambda: (pattern_main(0, 3), pattern_main(2, 0), pattern_main(0, 2)),
        (3, 3): lambda: (mats(6, 8), pattern_main(1, 1)),
        (3, 2): lambda: (pattern_main(1, 3), pattern_main(1, 2), mats(8, 9)),
        (2, 3): lambda: (mats(9, 11), pattern_main(3, 1)),
        (2, 2): lambda: (pattern_main(3, 3), pattern_main(3, 2), mats(11, 12)),
    }
    for oa in (1, 3, 2):
        for ob, lo, to, piece in ((1, 0, b_up, 0), (3, 8, b_dn, 1)):
            got_main(oa, ob, 0, 16, 0)
            send_main(oa, ob, lo, 8, to, oa, 2, piece)
            send_zb(oa, ob)
        fill[(oa, 3)]()
        got_main(oa, 2, 0, 8, 0)
        got_main(oa, 2, 8, 8, 1)
        send_zb(oa, 2)
        fill[(oa, 2)]()
    pattern_main(2, 1)
    pattern_main(2, 3)
    pattern_main(2, 2)
    for oa in (0, 1, 3, 2):
        pattern_zb(oa, 0)
        pattern_zb(oa, 1)

    load_rcv.wait()
    k_at = lax.broadcasted_iota(jnp.int32, (8, 384), 1) + pb * 384
    width = jnp.zeros((8, 384), jnp.int32)
    for i in range(32):
        lo, hi = offs[i], offs[i + 1]
        width = jnp.where((k_at >= lo) & (k_at < hi), hi - lo, width)
    weight = 1536.0 / (32.0 * width.astype(F32))
    rw[...] = (rcv[...].astype(F32) * weight[:1]).astype(BF)
    load_ns.wait()
    arrived(nsv, precv.at[1])
    load_ns2 = pltpu.make_async_copy(nsv, ns_par, lsem.at[5])
    load_ns2.start()
    load_ns2.wait()
    load_nb.wait()
    arrived(nb.at[pl.ds(oc * 6, 6)], precv.at[2])

    def near_boxes(ns, first, lo, hi):
        def box(i, _):
            w = first + i
            total = jnp.zeros((128, 128), F32)
            for m in range(0, 26, 2):
                blocks = jnp.concatenate([nb[w, m], nb[w, m + 1]], axis=1)
                fields = jnp.concatenate([cur[ns[i, m]], cur[ns[i, m + 1]]], axis=0)
                total += jnp.dot(blocks, fields, preferred_element_type=F32)
            total += jnp.dot(nb[w, 26], cur[ns[i, 26]], preferred_element_type=F32)
            acc[w] = total
            return 0

        lax.fori_loop(lo, hi, box, 0)

    own_copies = []

    def chunk(k):
        def one(i, _):
            t = k * TCH + i
            buf[pl.ds(i, 192, stride=TCH), :] = jnp.dot(mat[t], pat[t], preferred_element_type=F32)
            return 0

        lax.fori_loop(0, TCH, one, 0)

        def pack(i, _):
            v = buf[pl.ds(pl.multiple_of(i * 128, 128), 128), :]
            tx[pl.ds(i * 8, 8), k * TCH : (k + 1) * TCH, :] = v.reshape(8, TCH, 128).astype(BF)
            return 0

        lax.fori_loop(0, 24, pack, 0)
        ts = pl.ds(k * TCH, TCH)
        there = pl.ds(pl.multiple_of(pa * TB + k * TCH, TCH), TCH)
        far = m4(pa + 2) * 48
        go(remote(tx.at[pl.ds(far, 24), ts], relay.at[0, k], rsend.at[k * 6 + 2], rrecv.at[k * 6 + 2], a_up))
        go(remote(tx.at[pl.ds(far + 24, 24), ts], relay.at[1, k], rsend.at[k * 6 + 3], rrecv.at[k * 6 + 3], a_dn))
        go(remote(tx.at[pl.ds(m4(pa + 1) * 48, 48), ts], rx.at[:, there], rsend.at[k * 6], rrecv.at[k * 6], a_up))
        go(remote(tx.at[pl.ds(m4(pa - 1) * 48, 48), ts], rx.at[:, there], rsend.at[k * 6 + 1], rrecv.at[k * 6 + 1], a_dn))
        own = pltpu.make_async_copy(tx.at[pl.ds(pa * 48, 48), ts], rx.at[:, there], lsem.at[6 + k])
        own.start()
        own_copies.append(own)

    def rx_at(a_, k):
        return pl.ds(pl.multiple_of(a_ * TB + k * TCH, TCH), TCH)

    def forward(k):
        arrived(relay.at[0, k], rrecv.at[k * 6 + 2])
        go(remote(relay.at[0, k], rx.at[pl.ds(0, 24), rx_at(m4(pa - 1), k)],
                  rsend.at[k * 6 + 4], rrecv.at[k * 6 + 4], a_up))
        arrived(relay.at[1, k], rrecv.at[k * 6 + 3])
        go(remote(relay.at[1, k], rx.at[pl.ds(24, 24), rx_at(m4(pa + 1), k)],
                  rsend.at[k * 6 + 5], rrecv.at[k * 6 + 5], a_dn))

    chunk(0)
    chunk(1)
    forward(0)
    chunk(2)
    near_boxes(ns_own, c * 6, 0, 2)
    forward(1)
    chunk(3)
    near_boxes(ns_own, c * 6, 2, 4)
    forward(2)
    chunk(4)
    near_boxes(ns_own, c * 6, 4, 6)
    forward(3)
    chunk(5)
    near_boxes(ns_par, oc * 6, 0, 3)
    forward(4)
    near_boxes(ns_par, oc * 6, 3, 6)
    forward(5)
    for k in range(NCH):
        own_copies[k].wait()
        arrived(rx.at[:, rx_at(m4(pa - 1), k)], rrecv.at[k * 6])
        arrived(rx.at[:, rx_at(m4(pa + 1), k)], rrecv.at[k * 6 + 1])
        arrived(rx.at[pl.ds(0, 24), rx_at(m4(pa + 2), k)], rrecv.at[k * 6 + 4])
        arrived(rx.at[pl.ds(24, 24), rx_at(m4(pa + 2), k)], rrecv.at[k * 6 + 5])

    def contract(b_, put):
        def pair(i, _):
            j = b_ * 12 + 2 * i
            two = jnp.concatenate([rx[j], rx[j + 1]], axis=1)
            o = jnp.dot(rw[...], two, preferred_element_type=F32)
            put(2 * i, o[:, :128])
            put(2 * i + 1, o[:, 128:])
            return 0

        lax.fori_loop(0, 6, pair, 0)

    def put_ps(slot):
        def put(w, v):
            ps[slot, w] = v.astype(BF)

        return put

    def put_acc(w, v):
        acc[w] = acc[w] + v

    for o, to in ((2, b_far), (1, b_up), (3, b_dn)):
        contract(m4(pb + o), put_ps(o - 1))
        go(remote(ps.at[o - 1], pr.at[o - 1], ssend.at[o - 1], srecv.at[o - 1], to))
    contract(pb, put_acc)
    for o in (1, 3, 2):
        arrived(pr.at[o - 1], srecv.at[o - 1])

    def finish(first, slot):
        def one(i, _):
            w = first + i
            total = acc[w] + pr[0, w].astype(F32) + pr[1, w].astype(F32) + pr[2, w].astype(F32)
            fin[slot, i] = total.astype(BF)
            return 0

        lax.fori_loop(0, 6, one, 0)

    mine = pl.ds(pl.multiple_of(c * 128, 128), 128)
    theirs = pl.ds(pl.multiple_of(oc * 128, 128), 128)
    finish(oc * 6, 1)
    go(remote(fin.at[1], out.at[:, :, mine], psend.at[3], precv.at[3], partner))
    finish(c * 6, 0)
    write = pltpu.make_async_copy(fin.at[0], out.at[:, :, mine], lsem.at[12])
    write.start()
    write.wait()
    arrived(out.at[:, :, theirs], precv.at[3])
    for copy in pending:
        copy.wait_send()


def slots_of(s, swap, g):
    halo = (s < 96) | (s >= 288)
    i = jnp.where(s < 96, s + 96, jnp.where(s >= 288, s - 288, s - 96))
    chip = lax.shift_right_arithmetic(i * 5462, 16)
    w = i - 12 * chip
    y = lax.shift_right_arithmetic(chip, 2)
    x = chip & 3
    a = jnp.where(swap, y, x)
    b = jnp.where(swap, x, y)
    near_slot = (a * 4 + b) * 16 + w
    far_slot = 256 + ((a * 2 + (b & 1)) * 2 + (b >> 1)) * 8 + (w - 4)
    slot = jnp.where(halo, jnp.where(w < 4, near_slot + 12, far_slot), near_slot)
    gone = (s < 0) | ((g == 0) & (s < 96)) | ((g == 3) & (s >= 288))
    return jnp.where(gone, -1, slot)


def shards(currents, radiate, receive, transfer_table, near_blocks, dir_offsets, trans_src, trans_tid, near_src):
    d = lax.axis_index("dir")
    g = lax.axis_index("region")
    swap = (d & 1) == 1
    x, y = (d >> 1) & 3, d >> 3
    pa, pb = jnp.where(swap, y, x), jnp.where(swap, x, y)
    band = pb * 4 + pa
    tt_t = lax.dynamic_slice_in_dim(transfer_table, band * TB, TB, 1).T
    tt_t = jnp.pad(tt_t, ((0, 0), (0, 384 - tt_t.shape[1])))

    def paired(v):
        v = v.reshape(4, 4, 12, 48)
        v = jnp.where(swap, v, v.transpose(1, 0, 2, 3)).reshape(12, 2, 8, 48)
        v = jnp.pad(v, ((0, 0), (0, 0), (0, 0), (0, 16)), constant_values=-1)
        return jnp.concatenate([v[:, 0], v[:, 1]], axis=-1).reshape(96, 128)

    src = paired(slots_of(trans_src[0], swap, g))
    tid = paired(trans_tid[0])
    near = near_src[0]
    near = jnp.where(near < 0, -1, near + 48)

    def near_slots(turned):
        v = slots_of(near, turned, g)
        v = jnp.where(v < 0, 384, v)
        return jnp.pad(v, ((0, 2), (0, 101)), constant_values=384)

    nsl = jnp.concatenate([near_slots(swap), near_slots(~swap)], axis=0)
    any_spec = pl.BlockSpec(memory_space=pl.ANY)
    vmem = pl.BlockSpec(memory_space=pltpu.VMEM)
    dma = pltpu.SemaphoreType.DMA
    out = pl.pallas_call(
        body,
        out_shape=jax.ShapeDtypeStruct((6, 128, 256), BF),
        in_specs=[any_spec] * 5 + [vmem] * 3 + [pl.BlockSpec(memory_space=pltpu.SMEM)],
        out_specs=any_spec,
        scratch_shapes=[
            pltpu.VMEM((385, 128, 128), BF),
            pltpu.VMEM((12, 27, 128, 128), BF),
            pltpu.VMEM((TB, 192, 384), BF),
            pltpu.VMEM((TB, 384, 128), BF),
            pltpu.VMEM((192, TB, 128), BF),
            pltpu.VMEM((48, 4 * TB, 128), BF),
            pltpu.VMEM((2, NCH, 24, TCH, 128), BF),
            pltpu.VMEM((3, 12, 128, 128), BF),
            pltpu.VMEM((3, 12, 128, 128), BF),
            pltpu.VMEM((12, 128, 128), F32),
            pltpu.VMEM((3 * 1536, 128), F32),
            pltpu.VMEM((TB, 128), BF),
            pltpu.VMEM((128, 384), BF),
            pltpu.VMEM((128, 384), BF),
            pltpu.VMEM((2, 6, 128, 128), BF),
            pltpu.VMEM((8, 128), jnp.int32),
            pltpu.SMEM((8, 128), jnp.int32),
            pltpu.SMEM((8, 128), jnp.int32),
            dma((13,)),
            dma((4,)),
            dma((4,)),
            dma((48,)),
            dma((32,)),
            dma((17,)),
            dma((17,)),
            dma((36,)),
            dma((36,)),
            dma((3,)),
            dma((3,)),
        ],
        compiler_params=pltpu.CompilerParams(
            collective_id=0, has_side_effects=True, vmem_limit_bytes=67043328
        ),
        name="fmm",
    )(currents[0], radiate, receive, near_blocks[0], nsl, tt_t, src, tid, dir_offsets)
    return out[None]


def solution(mesh):
    placed = (
        P("region", "dir", None, None),
        P(),
        P(),
        P(),
        P("region", "dir", None, None, None),
        P(),
        P("region", None, None),
        P("region", None, None),
        P("region", "dir", None),
    )
    return jax.shard_map(
        shards,
        mesh=mesh,
        in_specs=placed,
        out_specs=P("region", "dir", None, None),
        check_vma=False,
    )
```

```python
import jax
import jax.numpy as jnp
from jax import lax
from jax.experimental import pallas as pl
from jax.experimental.pallas import tpu as pltpu
from jax.sharding import PartitionSpec as P

MESH = pl.DeviceIdType.MESH
BF = jnp.bfloat16
F32 = jnp.float32
TB = 96
NCH = 6
TCH = TB // 3


def m4(v):
    return lax.rem(v + 8, 4)


def body(
    cur_in, rad_in, rcv_in, nb_in, near_in, tt_in, src_in, tid_in, offs_in, out,
    cur, nb, mat, pat, tx, rx, relay, ps, pr, acc, bpat, bmat, btr, rad, rcv, rw, fin,
    near_v, near_m, ns, tts, wide, tt_t, sraw, stage, src, tid, offs,
    lsem, psend, precv, asend, arecv, zsend, zrecv, rsend, rrecv, ssend, srecv,
):
    d = lax.axis_index("dir")
    z = lax.axis_index("region")
    c = lax.rem(d, 2)
    chip = lax.div(d, 2)
    x = lax.rem(chip, 4)
    y = lax.div(chip, 4)
    pa = x + c * (y - x)
    pb = y + c * (x - y)
    oc = 1 - c

    def dev(a, b, zz=None):
        xx = a + c * (b - a)
        yy = b + c * (a - b)
        return ((yy * 4 + xx) * 2 + c, z if zz is None else zz)

    partner = (d + 1 - 2 * c, z)
    a_up, a_dn = dev(m4(pa + 1), pb), dev(m4(pa - 1), pb)
    b_up, b_dn = dev(pa, m4(pb + 1)), dev(pa, m4(pb - 1))
    b_far = dev(pa, m4(pb + 2))
    z_up, z_dn = dev(pa, pb, m4(z + 1)), dev(pa, pb, m4(z - 1))

    barrier = pltpu.get_barrier_semaphore()
    for peer in (z_up, z_dn, b_far, a_up, a_dn, b_up, b_dn, partner):
        pl.semaphore_signal(barrier, inc=1, device_id=peer, device_id_type=MESH)

    lane0 = pl.multiple_of(c * 128, 128)
    own_half = cur_in.at[:, :, pl.ds(lane0, 128)]

    def base(oa, ob):
        return pl.multiple_of((m4(pa - oa) * 4 + m4(pb - ob)) * 16, 16)

    own0 = base(0, 0)
    loads = {}

    def load(name, src_ref, dst_ref):
        loads[name] = pltpu.make_async_copy(src_ref, dst_ref, lsem.at[len(loads)])
        loads[name].start()

    load("keep", own_half, cur.at[pl.ds(own0, 6)])
    load("src", src_in, sraw.at[0])
    load("tid", tid_in, sraw.at[1])
    load("tt", tt_in.at[:, pl.ds(pl.multiple_of(pb * 384, 128), 384)], tts)
    load("rad", rad_in.at[pl.ds(pl.multiple_of((pb * 4 + pa) * TB, 16), TB)], rad)
    load("rcv", rcv_in.at[:, pl.ds(pl.multiple_of(pb * 384, 128), 384)], rcv)
    load("near", near_in, near_v.at[0])
    load("offs", offs_in, offs)

    pl.semaphore_wait(barrier, 8)
    pending = []

    def remote(src_ref, dst_ref, send, recv, to):
        return pltpu.make_async_remote_copy(
            src_ref=src_ref, dst_ref=dst_ref, send_sem=send, recv_sem=recv,
            device_id=to, device_id_type=MESH,
        )

    def go(copy):
        copy.start()
        pending.append(copy)

    def arrived(ref, sem):
        remote(ref, ref, psend.at[0], sem, partner).wait_recv()

    count = [0]

    def send_main(oa, ob, lo, n, to, ra, rb, piece, origin=None):
        part = cur.at[pl.ds(base(oa, ob) + lo, n)]
        go(remote(part if origin is None else origin, part,
                  asend.at[count[0]], arecv.at[(ra * 4 + rb) * 3 + piece], to))
        count[0] += 1

    def got_main(oa, ob, lo, n, piece):
        arrived(cur.at[pl.ds(base(oa, ob) + lo, n)], arecv.at[(oa * 4 + ob) * 3 + piece])

    def z_target(oa, ob):
        a_, b_ = m4(pa - oa), m4(pb - ob)
        yb = b_ + c * (a_ - b_)
        return dev(pa, pb, m4(z + 2 * lax.div(yb, 2) - 1))

    def zb_at(oa, ob):
        a_, b_ = m4(pa - oa), m4(pb - ob)
        return 256 + ((a_ * 2 + lax.rem(b_, 2)) * 2 + lax.div(b_, 2)) * 8

    def send_zb(oa, ob):
        go(remote(
            cur.at[pl.ds(base(oa, ob) + 4, 8)], cur.at[pl.ds(zb_at(oa, ob), 8)],
            zsend.at[oa * 4 + ob], zrecv.at[oa * 4 + ob], z_target(oa, ob),
        ))

    def got_zb(oa, ob):
        arrived(cur.at[pl.ds(zb_at(oa, ob), 8)], zrecv.at[oa * 4 + ob])

    def send_own(lo, n, piece, origin=None):
        send_main(0, 0, lo, n, a_up, 1, 0, piece, origin)
        send_main(0, 0, lo, n, a_dn, 3, 0, piece, origin)
        send_main(0, 0, lo, n, b_up, 0, 1, piece, origin)
        send_main(0, 0, lo, n, b_dn, 0, 3, piece, origin)

    go(remote(
        cur_in.at[:, :, pl.ds(pl.multiple_of(oc * 128, 128), 128)],
        cur.at[pl.ds((pb * 4 + pa) * 16 + 6, 6)], psend.at[0], precv.at[0], partner,
    ))
    go(remote(
        cur_in.at[pl.ds(0, 4), :, pl.ds(lane0, 128)], cur.at[pl.ds(own0 + 12, 4)],
        zsend.at[16], zrecv.at[16], z_target(0, 0),
    ))
    send_own(0, 6, 0, own_half)
    go(remote(near_in, near_v.at[1], psend.at[1], precv.at[1], partner))
    loads["keep"].wait()
    arrived(cur.at[pl.ds(own0 + 6, 6)], precv.at[0])
    send_own(6, 6, 1)
    send_zb(0, 0)
    arrived(cur.at[pl.ds(own0 + 12, 4)], zrecv.at[16])
    send_own(12, 4, 2)
    load("nb", nb_in, nb.at[pl.ds(0, 6)])
    go(remote(nb_in, nb.at[pl.ds(6, 6)], psend.at[2], precv.at[2], partner))
    cur[384] = jnp.zeros((128, 128), BF)

    def slot_of(s):
        halo = (s < 96) | (s >= 288)
        i = jnp.where(s < 96, s + 96, jnp.where(s >= 288, s - 288, s - 96))
        box_chip = lax.shift_right_arithmetic(i * 5462, 16)
        p = i - 12 * box_chip - 6 * c
        p = jnp.where(p < 0, p + 12, p)
        by = lax.shift_right_arithmetic(box_chip, 2)
        bx = box_chip - 4 * by
        a = bx + c * (by - bx)
        b = by + c * (bx - by)
        b_hi = lax.shift_right_arithmetic(b, 1)
        main = (a * 4 + b) * 16 + p
        beyond = 256 + ((a * 2 + b - 2 * b_hi) * 2 + b_hi) * 8 + (p - 4)
        slot = jnp.where(halo, jnp.where(p < 4, main + 12, beyond), main)
        low = jnp.where(z == 0, 96, 0)
        high = jnp.where(z == 3, 288, 384)
        return jnp.where((s < low) | (s >= high), -1, slot)

    def table(values, ref):
        stage[...] = jnp.full((128, 256), -1.0, F32)
        stage[0:48, 0:192] = values
        stage[64:112, 0:192] = values
        ref[0:128, :] = jnp.transpose(stage[:, 0:128])
        ref[128:256, :] = jnp.transpose(stage[:, 128:256])

    loads["src"].wait()
    table(slot_of(sraw[0]).astype(F32), src)
    loads["tid"].wait()
    table(sraw[1].astype(F32), tid)
    loads["tt"].wait()
    wide[...] = jnp.zeros((384, 384), F32)
    wide[0:316, :] = tts[...].astype(F32)
    tt_t[...] = jnp.transpose(wide[...]).astype(BF)
    loads["rad"].wait()

    def pattern_block(at):
        def pair(i, _):
            two = jnp.concatenate([cur[at + 2 * i], cur[at + 2 * i + 1]], axis=1)
            o = jnp.dot(rad[...], two, preferred_element_type=F32)
            bpat[2 * i] = o[:, :128].astype(BF)
            bpat[2 * i + 1] = o[:, 128:].astype(BF)
            return 0

        lax.fori_loop(0, 8, pair, 0)

        def turn(i, _):
            t0 = pl.multiple_of(i * 16, 16)
            pat[pl.ds(t0, 16), pl.ds(at, 16), :] = jnp.swapaxes(bpat[:, pl.ds(t0, 16), :], 0, 1)
            return 0

        lax.fori_loop(0, TB // 16, turn, 0, unroll=2)

    def patterns(*blocks):
        for oa, ob in blocks:
            pattern_block(base(oa, ob))

    def pattern_zb(oa, ob):
        got_zb(oa, ob)
        got_zb(oa, ob + 2)
        g = m4(pa - oa) * 2 + lax.rem(m4(pb - ob), 2)
        pattern_block(pl.multiple_of(256 + g * 16, 16))

    n_iota = lax.broadcasted_iota(jnp.int32, (384, 128), 0).astype(F32)
    lane = lax.broadcasted_iota(jnp.int32, (TB, 128), 1)

    def box_row(jp):
        group = lax.div(jp, 24)
        rest = jp - group * 24
        second = lax.div(rest, 12)
        p = rest - second * 12
        half = lax.div(group, 4)
        a_ = group - 4 * half
        b_ = m4(pb + jnp.where(half == 0, 2 - second, 3 - 3 * second))
        chip_ = (b_ + c * (a_ - b_)) * 4 + a_ + c * (b_ - a_)
        return chip_ * 12 + lax.rem(p + 6 * c, 12)

    def hot(ref, lo, hi):
        row = jnp.where(lane[:1] < 64, ref[pl.ds(lo, 1), :], ref[pl.ds(hi, 1), :])
        return jnp.where(n_iota == row, 1.0, 0.0).astype(BF)

    def mat_group(g):
        def two_rows(it, _):
            rows = [(box_row(g * 16 + 2 * it + p), box_row(g * 16 + 8 + 2 * it + p)) for p in range(2)]
            classes = jnp.concatenate([hot(tid, *rows[0]), hot(tid, *rows[1])], axis=1)
            coef = jnp.dot(
                tt_t[pl.ds(pl.multiple_of(pa * TB, 16), TB), :], classes, preferred_element_type=F32
            )
            for p in range(2):
                part = coef[:, p * 128 : (p + 1) * 128]
                both = jnp.concatenate(
                    [jnp.where(lane < 64, part, 0.0), jnp.where(lane < 64, 0.0, part)], axis=0
                ).astype(BF)
                placed = lax.dot_general(
                    both, hot(src, *rows[p]), (((1,), (1,)), ((), ())), preferred_element_type=F32
                )
                for h in range(2):
                    bmat[h * 8 + 2 * it + p] = placed[h * TB : (h + 1) * TB].astype(BF)
            return 0

        lax.fori_loop(0, 4, two_rows, 0)
        j0 = pl.multiple_of(g * 16, 16)

        def turn(i, _):
            t0 = pl.multiple_of(i * 16, 16)
            for q in range(3):
                lanes = slice(q * 128, (q + 1) * 128)
                mat[pl.ds(t0, 16), pl.ds(j0, 16), lanes] = jnp.swapaxes(bmat[:, pl.ds(t0, 16), lanes], 0, 1)
            return 0

        lax.fori_loop(0, TB // 16, turn, 0)

    def mats(lo, hi):
        lax.fori_loop(lo, hi, lambda g, _: (mat_group(g), 0)[1], 0)

    def line_event(oa):
        send_main(oa, 0, 0, 16, b_up, oa, 1, 0)
        send_main(oa, 0, 0, 16, b_dn, oa, 3, 0)

    for oa, ob in ((1, 0), (3, 0), (0, 1), (0, 3)):
        got_main(oa, ob, 0, 6, 0)
        got_main(oa, ob, 6, 6, 1)
        if (oa, ob) == (1, 0):
            send_main(1, 0, 0, 8, a_up, 2, 0, 0)
        if (oa, ob) == (0, 1):
            send_main(0, 1, 0, 8, b_up, 0, 2, 0)
        send_zb(oa, ob)
    got_main(3, 0, 12, 4, 2)
    send_main(3, 0, 8, 8, a_dn, 2, 0, 1)
    line_event(3)
    got_main(1, 0, 12, 4, 2)
    line_event(1)
    got_main(0, 3, 12, 4, 2)
    send_main(0, 3, 8, 8, b_dn, 0, 2, 1)
    got_main(0, 1, 12, 4, 2)
    mats(0, 1)
    patterns((0, 0))

    def halves(oa, ob):
        got_main(oa, ob, 0, 8, 0)
        got_main(oa, ob, 8, 8, 1)
        send_zb(oa, ob)

    def ring_event(oa):
        for ob, lo, to, piece in ((1, 0, b_up, 0), (3, 8, b_dn, 1)):
            got_main(oa, ob, 0, 16, 0)
            send_main(oa, ob, lo, 8, to, oa, 2, piece)
            send_zb(oa, ob)

    halves(2, 0)
    line_event(2)
    mats(1, 2)
    patterns((1, 0))
    ring_event(3)
    mats(2, 3)
    patterns((3, 0), (2, 0))
    ring_event(1)
    halves(0, 2)
    mats(3, 5)
    patterns((0, 1), (0, 3))
    ring_event(2)
    mats(5, 7)
    patterns((3, 1), (3, 3), (0, 2))
    halves(3, 2)
    mats(7, 9)
    patterns((1, 1), (1, 3))
    halves(1, 2)
    mats(9, 12)
    patterns((2, 1), (2, 3), (3, 2), (1, 2))
    halves(2, 2)
    patterns((2, 2))
    for oa, ob in ((0, 0), (0, 1), (3, 1), (1, 1), (3, 0), (1, 0), (2, 1), (2, 0)):
        pattern_zb(oa, ob)

    own_copies = []

    def chunk(h, k):
        n = h * 3 + k
        j0 = h * 96

        def one(i, _):
            t = k * TCH + i
            btr[i] = jnp.dot(mat[t, j0 : j0 + 96, :], pat[t], preferred_element_type=F32).astype(BF)
            return 0

        lax.fori_loop(0, TCH, one, 0, unroll=2)

        def pack(i, _):
            r0 = pl.multiple_of(lax.rem(i, 6) * 16, 16)
            t0 = pl.multiple_of(lax.div(i, 6) * 16, 16)
            tx[pl.ds(j0 + r0, 16), pl.ds(k * TCH + t0, 16), :] = jnp.swapaxes(
                btr[pl.ds(t0, 16), pl.ds(r0, 16), :], 0, 1
            )
            return 0

        lax.fori_loop(0, 12, pack, 0, unroll=2)
        ts = pl.ds(k * TCH, TCH)
        here = pl.ds(h * 24, 24)
        there = rx_at(pa, k)
        far = j0 + m4(pa + 2) * 24
        go(remote(tx.at[pl.ds(far, 12), ts], relay.at[0, n], rsend.at[n * 6 + 2], rrecv.at[n * 6 + 2], a_up))
        go(remote(tx.at[pl.ds(far + 12, 12), ts], relay.at[1, n], rsend.at[n * 6 + 3], rrecv.at[n * 6 + 3], a_dn))
        go(remote(tx.at[pl.ds(j0 + m4(pa + 1) * 24, 24), ts], rx.at[here, there], rsend.at[n * 6], rrecv.at[n * 6], a_up))
        go(remote(tx.at[pl.ds(j0 + m4(pa - 1) * 24, 24), ts], rx.at[here, there], rsend.at[n * 6 + 1], rrecv.at[n * 6 + 1], a_dn))
        own = pltpu.make_async_copy(tx.at[pl.ds(j0 + pa * 24, 24), ts], rx.at[here, there], lsem.at[10 + n])
        own.start()
        own_copies.append(own)

    def rx_at(a_, k):
        return pl.ds(pl.multiple_of(a_ * TB + k * TCH, TCH), TCH)

    def forward(h, k):
        n = h * 3 + k
        arrived(relay.at[0, n], rrecv.at[n * 6 + 2])
        go(remote(relay.at[0, n], rx.at[pl.ds(h * 24, 12), rx_at(m4(pa - 1), k)],
                  rsend.at[n * 6 + 4], rrecv.at[n * 6 + 4], a_up))
        arrived(relay.at[1, n], rrecv.at[n * 6 + 3])
        go(remote(relay.at[1, n], rx.at[pl.ds(h * 24 + 12, 12), rx_at(m4(pa + 1), k)],
                  rsend.at[n * 6 + 5], rrecv.at[n * 6 + 5], a_dn))

    def all_here(h):
        here = pl.ds(h * 24, 24)
        for k in range(3):
            n = h * 3 + k
            own_copies[n].wait()
            arrived(rx.at[here, rx_at(m4(pa - 1), k)], rrecv.at[n * 6])
            arrived(rx.at[here, rx_at(m4(pa + 1), k)], rrecv.at[n * 6 + 1])
            arrived(rx.at[pl.ds(h * 24, 12), rx_at(m4(pa + 2), k)], rrecv.at[n * 6 + 4])
            arrived(rx.at[pl.ds(h * 24 + 12, 12), rx_at(m4(pa + 2), k)], rrecv.at[n * 6 + 5])

    def near_boxes(which, lo, hi):
        def box(i, _):
            w = which * 6 + i
            total = jnp.zeros((128, 128), F32)
            for m in range(0, 26, 2):
                blocks = jnp.concatenate([nb[w, m], nb[w, m + 1]], axis=1)
                fields = jnp.concatenate([cur[ns[which, i, 0, m]], cur[ns[which, i, 0, m + 1]]], axis=0)
                total += jnp.dot(blocks, fields, preferred_element_type=F32)
            total += jnp.dot(nb[w, 26], cur[ns[which, i, 0, 26]], preferred_element_type=F32)
            acc[w] = total
            return 0

        lax.fori_loop(lo, hi, box, 0)

    def contract(group, put):
        def pair(i, _):
            j = group * 12 + 2 * i
            two = jnp.concatenate([rx[j], rx[j + 1]], axis=1)
            o = jnp.dot(rw[...], two, preferred_element_type=F32)
            put(2 * i, o[:, :128])
            put(2 * i + 1, o[:, 128:])
            return 0

        lax.fori_loop(0, 6, pair, 0)

    def partial_to(group, o, to):
        def put(w, v):
            ps[o - 1, w] = v.astype(BF)

        contract(group, put)
        go(remote(ps.at[o - 1], pr.at[o - 1], ssend.at[o - 1], srecv.at[o - 1], to))

    def put_acc(w, v):
        acc[w] = acc[w] + v

    chunk(0, 0)
    chunk(0, 1)
    forward(0, 0)
    chunk(0, 2)
    forward(0, 1)
    chunk(1, 0)
    loads["rcv"].wait()
    loads["offs"].wait()
    k_at = lax.broadcasted_iota(jnp.int32, (8, 384), 1) + pb * 384
    width = jnp.zeros((8, 384), jnp.int32)
    for i in range(32):
        lo, hi = offs[i], offs[i + 1]
        width = jnp.where((k_at >= lo) & (k_at < hi), hi - lo, width)
    weight = 1536.0 / (32.0 * width.astype(F32))
    rw[...] = (rcv[...].astype(F32) * weight[:1]).astype(BF)
    loads["near"].wait()
    arrived(near_v.at[1], precv.at[1])
    near_s = near_v[...]
    near_s = slot_of(jnp.where(near_s < 0, -1, near_s + 48))
    near_m[...] = jnp.where(near_s < 0, 384, near_s)
    forward(0, 2)
    load("ns", near_m, ns)
    chunk(1, 1)
    loads["ns"].wait()
    loads["nb"].wait()
    near_boxes(0, 0, 2)
    forward(1, 0)
    chunk(1, 2)
    all_here(0)
    partial_to(0, 2, b_far)
    partial_to(1, 1, b_up)
    forward(1, 1)
    near_boxes(0, 2, 5)
    forward(1, 2)
    near_boxes(0, 5, 6)
    arrived(nb.at[pl.ds(6, 6)], precv.at[2])
    near_boxes(1, 0, 6)
    all_here(1)
    partial_to(2, 3, b_dn)
    contract(3, put_acc)
    for o in (2, 1, 3):
        arrived(pr.at[o - 1], srecv.at[o - 1])

    def finish(which):
        def one(i, _):
            w = which * 6 + i
            total = acc[w] + pr[0, w].astype(F32) + pr[1, w].astype(F32) + pr[2, w].astype(F32)
            fin[which, i] = total.astype(BF)
            return 0

        lax.fori_loop(0, 6, one, 0)

    mine = pl.ds(lane0, 128)
    theirs = pl.ds(pl.multiple_of(oc * 128, 128), 128)
    finish(1)
    go(remote(fin.at[1], out.at[:, :, mine], psend.at[3], precv.at[3], partner))
    finish(0)
    write = pltpu.make_async_copy(fin.at[0], out.at[:, :, mine], lsem.at[16])
    write.start()
    write.wait()
    arrived(out.at[:, :, theirs], precv.at[3])
    for copy in pending:
        copy.wait_send()


def shards(currents, radiate, receive, transfer_table, near_blocks, dir_offsets, trans_src, trans_tid, near_src):
    any_spec = pl.BlockSpec(memory_space=pl.ANY)
    dma = pltpu.SemaphoreType.DMA
    out = pl.pallas_call(
        body,
        out_shape=jax.ShapeDtypeStruct((6, 128, 256), BF),
        in_specs=[any_spec] * 9,
        out_specs=any_spec,
        scratch_shapes=[
            pltpu.VMEM((385, 128, 128), BF),
            pltpu.VMEM((12, 27, 128, 128), BF),
            pltpu.VMEM((TB, 192, 384), BF),
            pltpu.VMEM((TB, 384, 128), BF),
            pltpu.VMEM((192, TB, 128), BF),
            pltpu.VMEM((48, 4 * TB, 128), BF),
            pltpu.VMEM((2, NCH, 12, TCH, 128), BF),
            pltpu.VMEM((3, 12, 128, 128), BF),
            pltpu.VMEM((3, 12, 128, 128), BF),
            pltpu.VMEM((12, 128, 128), F32),
            pltpu.VMEM((16, TB, 128), BF),
            pltpu.VMEM((16, TB, 384), BF),
            pltpu.VMEM((TCH, 96, 128), BF),
            pltpu.VMEM((TB, 128), BF),
            pltpu.VMEM((128, 384), BF),
            pltpu.VMEM((128, 384), BF),
            pltpu.VMEM((2, 6, 128, 128), BF),
            pltpu.VMEM((2, 6, 1, 27), jnp.int32),
            pltpu.VMEM((2, 6, 1, 27), jnp.int32),
            pltpu.SMEM((2, 6, 1, 27), jnp.int32),
            pltpu.VMEM((316, 384), BF),
            pltpu.VMEM((384, 384), F32),
            pltpu.VMEM((384, 384), BF),
            pltpu.VMEM((2, 48, 192), jnp.int32),
            pltpu.VMEM((128, 256), F32),
            pltpu.VMEM((256, 128), F32),
            pltpu.VMEM((256, 128), F32),
            pltpu.SMEM((33,), jnp.int32),
            dma((17,)),
            dma((4,)),
            dma((4,)),
            dma((48,)),
            dma((48,)),
            dma((17,)),
            dma((17,)),
            dma((36,)),
            dma((36,)),
            dma((3,)),
            dma((3,)),
        ],
        compiler_params=pltpu.CompilerParams(
            collective_id=0, has_side_effects=True, vmem_limit_bytes=67043328
        ),
        name="fmm",
    )(
        currents[0], radiate, receive, near_blocks[0], jnp.swapaxes(near_src, 0, 1), transfer_table,
        jnp.swapaxes(trans_src[0], 0, 1), jnp.swapaxes(trans_tid[0], 0, 1), dir_offsets,
    )
    return out[None]


def solution(mesh):
    placed = (
        P("region", "dir", None, None),
        P(),
        P(),
        P(),
        P("region", "dir", None, None, None),
        P(),
        P("region", None, None),
        P("region", None, None),
        P("region", "dir", None),
    )
    return jax.shard_map(
        shards,
        mesh=mesh,
        in_specs=placed,
        out_specs=P("region", "dir", None, None),
        check_vma=False,
    )
```

```python
import jax
import jax.numpy as jnp
from jax import lax
from jax.experimental import pallas as pl
from jax.experimental.pallas import tpu as pltpu
from jax.sharding import PartitionSpec as P

MESH = pl.DeviceIdType.MESH
BF = jnp.bfloat16
F32 = jnp.float32
TB = 96
NCH = 6
TCH = TB // 3


def m4(v):
    return lax.rem(v + 8, 4)


def body(
    cur_in, rad_in, rcv_in, nb_in, near_in, tt_in, src_in, tid_in, offs_in, out,
    cur, nb, mat, pat, tx, rx, relay, hop, ps, pr, acc, bpat, bmat, btr, rad, rcv, rw, fin,
    near_v, near_m, ns, tts, wide, tt_t, sraw, stage, src, tid, offs,
    lsem, psend, precv, asend, arecv, zsend, zrecv, rsend, rrecv, ssend, srecv,
):
    d = lax.axis_index("dir")
    z = lax.axis_index("region")
    c = lax.rem(d, 2)
    chip = lax.div(d, 2)
    x = lax.rem(chip, 4)
    y = lax.div(chip, 4)
    pa = x + c * (y - x)
    pb = y + c * (x - y)
    oc = 1 - c

    def dev(a, b, zz=None):
        xx = a + c * (b - a)
        yy = b + c * (a - b)
        return ((yy * 4 + xx) * 2 + c, z if zz is None else zz)

    partner = (d + 1 - 2 * c, z)
    a_up, a_dn = dev(m4(pa + 1), pb), dev(m4(pa - 1), pb)
    b_up, b_dn = dev(pa, m4(pb + 1)), dev(pa, m4(pb - 1))
    z_up, z_dn = dev(pa, pb, m4(z + 1)), dev(pa, pb, m4(z - 1))

    barrier = pltpu.get_barrier_semaphore()
    for peer in (z_up, z_dn, a_up, a_dn, b_up, b_dn, partner):
        pl.semaphore_signal(barrier, inc=1, device_id=peer, device_id_type=MESH)

    lane0 = pl.multiple_of(c * 128, 128)
    own_half = cur_in.at[:, :, pl.ds(lane0, 128)]

    def base(oa, ob):
        return (m4(pa - oa) * 4 + m4(pb - ob)) * 18

    own0 = base(0, 0)
    loads = {}

    def load(name, src_ref, dst_ref):
        loads[name] = pltpu.make_async_copy(src_ref, dst_ref, lsem.at[len(loads)])
        loads[name].start()

    load("keep", own_half, cur.at[pl.ds(own0, 6)])
    load("src", src_in, sraw.at[0])
    load("tid", tid_in, sraw.at[1])
    load("tt", tt_in.at[:, pl.ds(pl.multiple_of(pb * 384, 128), 384)], tts)
    load("rad", rad_in.at[pl.ds(pl.multiple_of((pb * 4 + pa) * TB, 16), TB)], rad)
    load("rcv", rcv_in.at[:, pl.ds(pl.multiple_of(pb * 384, 128), 384)], rcv)
    load("near", near_in, near_v.at[0])
    load("offs", offs_in, offs)

    pl.semaphore_wait(barrier, 7)
    pending = []

    def remote(src_ref, dst_ref, send, recv, to):
        return pltpu.make_async_remote_copy(
            src_ref=src_ref, dst_ref=dst_ref, send_sem=send, recv_sem=recv,
            device_id=to, device_id_type=MESH,
        )

    def go(copy):
        copy.start()
        pending.append(copy)

    def arrived(ref, sem):
        remote(ref, ref, psend.at[0], sem, partner).wait_recv()

    count = [0]

    def send_main(oa, ob, lo, n, to, ra, rb, piece, origin=None):
        part = cur.at[pl.ds(base(oa, ob) + lo, n)]
        go(remote(part if origin is None else origin, part,
                  asend.at[count[0]], arecv.at[(ra * 4 + rb) * 3 + piece], to))
        count[0] += 1

    def got_main(oa, ob, lo, n, piece):
        arrived(cur.at[pl.ds(base(oa, ob) + lo, n)], arecv.at[(oa * 4 + ob) * 3 + piece])

    def z_target(oa, ob):
        a_, b_ = m4(pa - oa), m4(pb - ob)
        yb = b_ + c * (a_ - b_)
        return dev(pa, pb, m4(z + 2 * lax.div(yb, 2) - 1))

    def zb_at(oa, ob):
        a_, b_ = m4(pa - oa), m4(pb - ob)
        return 288 + ((a_ * 2 + lax.rem(b_, 2)) * 2 + lax.div(b_, 2)) * 6

    def send_zb(oa, ob):
        go(remote(
            cur.at[pl.ds(base(oa, ob) + 6, 6)], cur.at[pl.ds(zb_at(oa, ob), 6)],
            zsend.at[oa * 4 + ob], zrecv.at[oa * 4 + ob], z_target(oa, ob),
        ))

    def got_zb(oa, ob):
        arrived(cur.at[pl.ds(zb_at(oa, ob), 6)], zrecv.at[oa * 4 + ob])

    def send_own(lo, n, piece, origin=None):
        send_main(0, 0, lo, n, a_up, 1, 0, piece, origin)
        send_main(0, 0, lo, n, a_dn, 3, 0, piece, origin)
        send_main(0, 0, lo, n, b_up, 0, 1, piece, origin)
        send_main(0, 0, lo, n, b_dn, 0, 3, piece, origin)

    go(remote(
        cur_in.at[:, :, pl.ds(pl.multiple_of(oc * 128, 128), 128)],
        cur.at[pl.ds((pb * 4 + pa) * 18 + 6, 6)], psend.at[0], precv.at[0], partner,
    ))
    go(remote(
        own_half, cur.at[pl.ds(own0 + 12, 6)],
        zsend.at[16], zrecv.at[16], z_target(0, 0),
    ))
    send_own(0, 6, 0, own_half)
    go(remote(near_in, near_v.at[1], psend.at[1], precv.at[1], partner))
    loads["keep"].wait()
    arrived(cur.at[pl.ds(own0 + 6, 6)], precv.at[0])
    send_own(6, 6, 1)
    send_zb(0, 0)
    arrived(cur.at[pl.ds(own0 + 12, 6)], zrecv.at[16])
    send_own(12, 6, 2)
    load("nb", nb_in, nb.at[pl.ds(0, 6)])
    go(remote(nb_in, nb.at[pl.ds(6, 6)], psend.at[2], precv.at[2], partner))
    cur[384] = jnp.zeros((128, 128), BF)

    def slot_of(s, field):
        halo = (s < 96) | (s >= 288)
        i = jnp.where(s < 96, s + 96, jnp.where(s >= 288, s - 288, s - 96))
        box_chip = lax.shift_right_arithmetic(i * 5462, 16)
        p = i - 12 * box_chip - 6 * c
        p = jnp.where(p < 0, p + 12, p)
        by = lax.shift_right_arithmetic(box_chip, 2)
        bx = box_chip - 4 * by
        a = bx + c * (by - bx)
        b = by + c * (bx - by)
        b_hi = lax.shift_right_arithmetic(b, 1)
        size, rim = (18, 6) if field else (16, 4)
        main = (a * 4 + b) * size + p
        beyond = 16 * size + ((a * 2 + b - 2 * b_hi) * 2 + b_hi) * (12 - rim) + (p - rim)
        slot = jnp.where(halo, jnp.where(p < rim, main + 12, beyond), main)
        low = jnp.where(z == 0, 96, 0)
        high = jnp.where(z == 3, 288, 384)
        return jnp.where((s < low) | (s >= high), -1, slot)

    def table(values, ref):
        stage[...] = jnp.full((128, 256), -1.0, F32)
        stage[0:48, 0:192] = values
        stage[64:112, 0:192] = values
        ref[0:128, :] = jnp.transpose(stage[:, 0:128])
        ref[128:256, :] = jnp.transpose(stage[:, 128:256])

    loads["src"].wait()
    table(slot_of(sraw[0], False).astype(F32), src)
    loads["tid"].wait()
    table(sraw[1].astype(F32), tid)
    loads["tt"].wait()
    wide[...] = jnp.zeros((384, 384), F32)
    wide[0:316, :] = tts[...].astype(F32)
    tt_t[...] = jnp.transpose(wide[...]).astype(BF)
    loads["rad"].wait()

    def pattern_block(at, box):
        for i in range(8):
            two = jnp.concatenate([cur[box(2 * i)], cur[box(2 * i + 1)]], axis=1)
            o = jnp.dot(rad[...], two, preferred_element_type=F32)
            bpat[2 * i] = o[:, :128].astype(BF)
            bpat[2 * i + 1] = o[:, 128:].astype(BF)

        def turn(i, _):
            t0 = pl.multiple_of(i * 16, 16)
            pat[pl.ds(t0, 16), pl.ds(at, 16), :] = jnp.swapaxes(bpat[:, pl.ds(t0, 16), :], 0, 1)
            return 0

        lax.fori_loop(0, TB // 16, turn, 0, unroll=2)

    def patterns(*blocks):
        for oa, ob in blocks:
            first = base(oa, ob)
            at = (m4(pa - oa) * 4 + m4(pb - ob)) * 16
            pattern_block(pl.multiple_of(at, 16), lambda i, first=first: first + i)

    def pattern_zb(oa, ob):
        got_zb(oa, ob)
        got_zb(oa, ob + 2)
        a_, parity = m4(pa - oa), lax.rem(m4(pb - ob), 2)
        g = a_ * 2 + parity
        rim0 = (a_ * 4 + parity) * 18 + 16
        over0 = 288 + g * 12

        def box(i):
            second, q = i // 8, i % 8
            return rim0 + second * 36 + q if q < 2 else over0 + second * 6 + q - 2

        pattern_block(pl.multiple_of(256 + g * 16, 16), box)

    n_iota = lax.broadcasted_iota(jnp.int32, (384, 128), 0).astype(F32)
    lane = lax.broadcasted_iota(jnp.int32, (TB, 128), 1)

    def box_row(jp):
        late = jnp.where(jp >= 144, 1, 0)
        at = jp - 144 * late
        size = 36 - 24 * late
        a_ = lax.div(at * (1 + 2 * late), 36)
        rest = at - a_ * size
        which = lax.div(rest, 12)
        p = rest - which * 12
        b_ = m4(pb + jnp.where(late == 1, 0, jnp.where(which == 2, 3, 2 - which)))
        chip_ = (b_ + c * (a_ - b_)) * 4 + a_ + c * (b_ - a_)
        return chip_ * 12 + lax.rem(p + 6 * c, 12)

    def hot(ref, lo, hi):
        row = jnp.where(lane[:1] < 64, ref[pl.ds(lo, 1), :], ref[pl.ds(hi, 1), :])
        return jnp.where(n_iota == row, 1.0, 0.0).astype(BF)

    def mat_group(g):
        def two_rows(it, _):
            rows = [(box_row(g * 16 + 2 * it + p), box_row(g * 16 + 8 + 2 * it + p)) for p in range(2)]
            classes = jnp.concatenate([hot(tid, *rows[0]), hot(tid, *rows[1])], axis=1)
            coef = jnp.dot(
                tt_t[pl.ds(pl.multiple_of(pa * TB, 16), TB), :], classes, preferred_element_type=F32
            )
            for p in range(2):
                part = coef[:, p * 128 : (p + 1) * 128]
                both = jnp.concatenate(
                    [jnp.where(lane < 64, part, 0.0), jnp.where(lane < 64, 0.0, part)], axis=0
                ).astype(BF)
                placed = lax.dot_general(
                    both, hot(src, *rows[p]), (((1,), (1,)), ((), ())), preferred_element_type=F32
                )
                for h in range(2):
                    bmat[h * 8 + 2 * it + p] = placed[h * TB : (h + 1) * TB].astype(BF)
            return 0

        lax.fori_loop(0, 4, two_rows, 0, unroll=4)
        j0 = pl.multiple_of(g * 16, 16)

        def turn(i, _):
            t0 = pl.multiple_of(i * 16, 16)
            for q in range(3):
                lanes = slice(q * 128, (q + 1) * 128)
                mat[pl.ds(t0, 16), pl.ds(j0, 16), lanes] = jnp.swapaxes(bmat[:, pl.ds(t0, 16), lanes], 0, 1)
            return 0

        lax.fori_loop(0, TB // 16, turn, 0)

    def mats(lo, hi):
        lax.fori_loop(lo, hi, lambda g, _: (mat_group(g), 0)[1], 0)

    def line_event(oa):
        send_main(oa, 0, 0, 18, b_up, oa, 1, 0)
        send_main(oa, 0, 0, 18, b_dn, oa, 3, 0)

    odd = lax.rem(y, 2)
    line1 = 3 - 2 * c * (1 - odd)
    line2 = 1 + c
    line3 = 2 + c * (1 - 2 * odd)

    def halves(oa, ob):
        got_main(oa, ob, 0, 9, 0)
        got_main(oa, ob, 9, 9, 1)
        send_zb(oa, ob)

    def ring_event(oa):
        for ob, lo, to, piece in ((1, 0, b_up, 0), (3, 9, b_dn, 1)):
            got_main(oa, ob, 0, 18, 0)
            send_main(oa, ob, lo, 9, to, oa, 2, piece)
            send_zb(oa, ob)

    for oa, ob in ((1, 0), (3, 0), (0, 1), (0, 3)):
        got_main(oa, ob, 0, 6, 0)
        got_main(oa, ob, 6, 6, 1)
        if (oa, ob) == (1, 0):
            send_main(1, 0, 0, 9, a_up, 2, 0, 0)
        if (oa, ob) == (0, 1):
            send_main(0, 1, 0, 9, b_up, 0, 2, 0)
        send_zb(oa, ob)
    got_main(3, 0, 12, 6, 2)
    send_main(3, 0, 9, 9, a_dn, 2, 0, 1)
    got_main(1, 0, 12, 6, 2)
    line_event(line1)
    got_main(0, 3, 12, 6, 2)
    send_main(0, 3, 9, 9, b_dn, 0, 2, 1)
    got_main(0, 1, 12, 6, 2)
    mats(0, 1)
    patterns((0, 0))
    halves(2, 0)
    line_event(line2)
    line_event(line3)
    mats(1, 2)
    patterns((1, 0))
    ring_event(line1)
    mats(2, 3)
    patterns((3, 0), (2, 0))
    halves(0, 2)
    mats(3, 5)
    patterns((0, 1), (0, 3))
    ring_event(line2)
    mats(5, 7)
    patterns((line1, 1), (line1, 3), (0, 2))
    halves(line1, 2)
    mats(7, 9)
    patterns((line2, 1), (line2, 3))
    ring_event(line3)
    mats(9, 12)
    halves(line2, 2)
    patterns((line3, 1), (line3, 3), (line1, 2), (line2, 2))
    halves(line3, 2)
    patterns((line3, 2))
    for oa, ob in (
        (0, 0), (0, 1), (line1, 1), (line1, 0), (line2, 1), (line2, 0), (line3, 1), (line3, 0)
    ):
        pattern_zb(oa, ob)

    first_row, rows_of = (0, 144), (36, 12)
    own_copies = []

    def chunk(h, k):
        n = h * 3 + k
        j0, n_rows = first_row[h], rows_of[h]
        n_half, n_tiles = n_rows // 2, n_rows // 4

        def one(i, _):
            t = k * TCH + i
            o = jnp.dot(mat[t, j0 : j0 + 4 * n_rows, :], pat[t], preferred_element_type=F32)
            btr[i, 0 : 4 * n_rows] = o.astype(BF)
            return 0

        lax.fori_loop(0, TCH, one, 0, unroll=8)

        def pack(i, _):
            r0 = pl.multiple_of(lax.rem(i, n_tiles) * 16, 16)
            t0 = pl.multiple_of(lax.div(i, n_tiles) * 16, 16)
            tx[pl.ds(j0 + r0, 16), pl.ds(k * TCH + t0, 16), :] = jnp.swapaxes(
                btr[pl.ds(t0, 16), pl.ds(r0, 16), :], 0, 1
            )
            return 0

        lax.fori_loop(0, 2 * n_tiles, pack, 0, unroll=2)
        ts = pl.ds(k * TCH, TCH)
        here = pl.ds(h * 36, n_rows)
        there = rx_at(pa, k)
        far = j0 + m4(pa + 2) * n_rows
        hop_rows = pl.ds(0, n_half)
        go(remote(tx.at[pl.ds(far, n_half), ts], relay.at[0, n, hop_rows], rsend.at[n * 6 + 2], rrecv.at[n * 6 + 2], a_up))
        go(remote(tx.at[pl.ds(far + n_half, n_half), ts], relay.at[1, n, hop_rows], rsend.at[n * 6 + 3], rrecv.at[n * 6 + 3], a_dn))
        go(remote(tx.at[pl.ds(j0 + m4(pa + 1) * n_rows, n_rows), ts], rx.at[here, there], rsend.at[n * 6], rrecv.at[n * 6], a_up))
        go(remote(tx.at[pl.ds(j0 + m4(pa - 1) * n_rows, n_rows), ts], rx.at[here, there], rsend.at[n * 6 + 1], rrecv.at[n * 6 + 1], a_dn))
        own = pltpu.make_async_copy(tx.at[pl.ds(j0 + pa * n_rows, n_rows), ts], rx.at[here, there], lsem.at[10 + n])
        own.start()
        own_copies.append(own)

    def rx_at(a_, k):
        return pl.ds(pl.multiple_of(a_ * TB + k * TCH, TCH), TCH)

    def forward(h, k):
        n = h * 3 + k
        n_half = rows_of[h] // 2
        for way, o, to in ((0, -1, a_up), (1, 1, a_dn)):
            held = relay.at[way, n, pl.ds(0, n_half)]
            arrived(held, rrecv.at[n * 6 + 2 + way])
            go(remote(held, rx.at[pl.ds(h * 36 + way * n_half, n_half), rx_at(m4(pa + o), k)],
                      rsend.at[n * 6 + 4 + way], rrecv.at[n * 6 + 4 + way], to))

    def all_here(h):
        n_half = rows_of[h] // 2
        here = pl.ds(h * 36, 2 * n_half)
        for k in range(3):
            n = h * 3 + k
            own_copies[n].wait()
            arrived(rx.at[here, rx_at(m4(pa - 1), k)], rrecv.at[n * 6])
            arrived(rx.at[here, rx_at(m4(pa + 1), k)], rrecv.at[n * 6 + 1])
            for way in range(2):
                arrived(rx.at[pl.ds(h * 36 + way * n_half, n_half), rx_at(m4(pa + 2), k)],
                        rrecv.at[n * 6 + 4 + way])

    def near_boxes(which, lo, hi):
        def box(i, _):
            w = which * 6 + i
            total = jnp.zeros((128, 128), F32)
            for m in range(0, 26, 2):
                blocks = jnp.concatenate([nb[w, m], nb[w, m + 1]], axis=1)
                fields = jnp.concatenate([cur[ns[which, i, 0, m]], cur[ns[which, i, 0, m + 1]]], axis=0)
                total += jnp.dot(blocks, fields, preferred_element_type=F32)
            total += jnp.dot(nb[w, 26], cur[ns[which, i, 0, 26]], preferred_element_type=F32)
            acc[w] = total
            return 0

        lax.fori_loop(lo, hi, box, 0)

    def contract(group, put):
        def pair(i, _):
            j = group * 12 + 2 * i
            two = jnp.concatenate([rx[j], rx[j + 1]], axis=1)
            o = jnp.dot(rw[...], two, preferred_element_type=F32)
            put(2 * i, o[:, :128])
            put(2 * i + 1, o[:, 128:])
            return 0

        lax.fori_loop(0, 6, pair, 0)

    def partial_to(group, o, to):
        def put(w, v):
            ps[o - 1, w] = v.astype(BF)

        contract(group, put)
        go(remote(ps.at[o - 1], pr.at[o - 1], ssend.at[o - 1], srecv.at[o - 1], to))

    def put_acc(w, v):
        acc[w] = acc[w] + v

    chunk(0, 0)
    chunk(0, 1)
    forward(0, 0)
    chunk(0, 2)
    loads["rcv"].wait()
    loads["offs"].wait()
    k_at = lax.broadcasted_iota(jnp.int32, (8, 384), 1) + pb * 384
    width = jnp.zeros((8, 384), jnp.int32)
    for i in range(32):
        lo, hi = offs[i], offs[i + 1]
        width = jnp.where((k_at >= lo) & (k_at < hi), hi - lo, width)
    weight = 1536.0 / (32.0 * width.astype(F32))
    rw[...] = (rcv[...].astype(F32) * weight[:1]).astype(BF)
    loads["near"].wait()
    arrived(near_v.at[1], precv.at[1])
    near_s = near_v[...]
    near_s = slot_of(jnp.where(near_s < 0, -1, near_s + 48), True)
    near_m[...] = jnp.where(near_s < 0, 384, near_s)
    forward(0, 1)
    load("ns", near_m, ns)
    chunk(1, 0)
    chunk(1, 1)
    forward(0, 2)
    chunk(1, 2)
    loads["ns"].wait()
    loads["nb"].wait()
    near_boxes(0, 0, 4)
    forward(1, 0)
    all_here(0)

    def put_far(w, v):
        ps[1, w] = v.astype(BF)

    contract(0, put_far)
    go(remote(ps.at[1, pl.ds(0, 6)], hop.at[0], ssend.at[1], srecv.at[1], b_up))
    go(remote(ps.at[1, pl.ds(6, 6)], hop.at[1], ssend.at[3], srecv.at[3], b_dn))
    partial_to(1, 1, b_up)
    partial_to(2, 3, b_dn)
    forward(1, 1)
    arrived(hop.at[0], srecv.at[1])
    go(remote(hop.at[0], pr.at[1, pl.ds(0, 6)], ssend.at[4], srecv.at[4], b_up))
    arrived(hop.at[1], srecv.at[3])
    go(remote(hop.at[1], pr.at[1, pl.ds(6, 6)], ssend.at[5], srecv.at[5], b_dn))
    forward(1, 2)
    near_boxes(0, 4, 6)
    arrived(nb.at[pl.ds(6, 6)], precv.at[2])
    near_boxes(1, 0, 6)
    all_here(1)
    contract(3, put_acc)
    arrived(pr.at[0], srecv.at[0])
    arrived(pr.at[2], srecv.at[2])
    arrived(pr.at[1, pl.ds(0, 6)], srecv.at[4])
    arrived(pr.at[1, pl.ds(6, 6)], srecv.at[5])

    def finish(which):
        def one(i, _):
            w = which * 6 + i
            total = acc[w] + pr[0, w].astype(F32) + pr[1, w].astype(F32) + pr[2, w].astype(F32)
            fin[which, i] = total.astype(BF)
            return 0

        lax.fori_loop(0, 6, one, 0)

    mine = pl.ds(lane0, 128)
    theirs = pl.ds(pl.multiple_of(oc * 128, 128), 128)
    finish(1)
    go(remote(fin.at[1], out.at[:, :, mine], psend.at[3], precv.at[3], partner))
    finish(0)
    write = pltpu.make_async_copy(fin.at[0], out.at[:, :, mine], lsem.at[16])
    write.start()
    write.wait()
    arrived(out.at[:, :, theirs], precv.at[3])
    for copy in pending:
        copy.wait_send()


def shards(currents, radiate, receive, transfer_table, near_blocks, dir_offsets, trans_src, trans_tid, near_src):
    any_spec = pl.BlockSpec(memory_space=pl.ANY)
    dma = pltpu.SemaphoreType.DMA
    out = pl.pallas_call(
        body,
        out_shape=jax.ShapeDtypeStruct((6, 128, 256), BF),
        in_specs=[any_spec] * 9,
        out_specs=any_spec,
        scratch_shapes=[
            pltpu.VMEM((385, 128, 128), BF),
            pltpu.VMEM((12, 27, 128, 128), BF),
            pltpu.VMEM((TB, 192, 384), BF),
            pltpu.VMEM((TB, 384, 128), BF),
            pltpu.VMEM((192, TB, 128), BF),
            pltpu.VMEM((48, 4 * TB, 128), BF),
            pltpu.VMEM((2, NCH, 18, TCH, 128), BF),
            pltpu.VMEM((2, 6, 128, 128), BF),
            pltpu.VMEM((3, 12, 128, 128), BF),
            pltpu.VMEM((3, 12, 128, 128), BF),
            pltpu.VMEM((12, 128, 128), F32),
            pltpu.VMEM((16, TB, 128), BF),
            pltpu.VMEM((16, TB, 384), BF),
            pltpu.VMEM((TCH, 144, 128), BF),
            pltpu.VMEM((TB, 128), BF),
            pltpu.VMEM((128, 384), BF),
            pltpu.VMEM((128, 384), BF),
            pltpu.VMEM((2, 6, 128, 128), BF),
            pltpu.VMEM((2, 6, 1, 27), jnp.int32),
            pltpu.VMEM((2, 6, 1, 27), jnp.int32),
            pltpu.SMEM((2, 6, 1, 27), jnp.int32),
            pltpu.VMEM((316, 384), BF),
            pltpu.VMEM((384, 384), F32),
            pltpu.VMEM((384, 384), BF),
            pltpu.VMEM((2, 48, 192), jnp.int32),
            pltpu.VMEM((128, 256), F32),
            pltpu.VMEM((256, 128), F32),
            pltpu.VMEM((256, 128), F32),
            pltpu.SMEM((33,), jnp.int32),
            dma((17,)),
            dma((4,)),
            dma((4,)),
            dma((48,)),
            dma((48,)),
            dma((17,)),
            dma((17,)),
            dma((36,)),
            dma((36,)),
            dma((6,)),
            dma((6,)),
        ],
        compiler_params=pltpu.CompilerParams(
            collective_id=0, has_side_effects=True, vmem_limit_bytes=67043328
        ),
        name="fmm",
    )(
        currents[0], radiate, receive, near_blocks[0], jnp.swapaxes(near_src, 0, 1), transfer_table,
        jnp.swapaxes(trans_src[0], 0, 1), jnp.swapaxes(trans_tid[0], 0, 1), dir_offsets,
    )
    return out[None]


def solution(mesh):
    placed = (
        P("region", "dir", None, None),
        P(),
        P(),
        P(),
        P("region", "dir", None, None, None),
        P(),
        P("region", None, None),
        P("region", None, None),
        P("region", "dir", None),
    )
    return jax.shard_map(
        shards,
        mesh=mesh,
        in_specs=placed,
        out_specs=P("region", "dir", None, None),
        check_vma=False,
    )
```

```python
import jax
import jax.numpy as jnp
from jax import lax
from jax.experimental import pallas as pl
from jax.experimental.pallas import tpu as pltpu
from jax.sharding import PartitionSpec as P

MESH = pl.DeviceIdType.MESH
BF = jnp.bfloat16
F32 = jnp.float32
TB = 96
NCH = 6
TCH = TB // 3
RIM = 6
BLK = 12 + RIM
HALF = (BLK + 1) // 2


def m4(v):
    return lax.rem(v + 8, 4)


def body(
    cur_in, rad_in, rcv_in, nb_in, near_in, tt_in, src_in, tid_in, offs_in, out,
    cur, nb, mat, pat, tx, rx, relay, hop, ps, pr, acc, bpat, bmat, btr, rad, rcv, rw, fin,
    near_v, near_m, ns, tts, wide, tt_t, sraw, stage, src, tid, offs,
    lsem, psend, precv, asend, arecv, zsend, zrecv, rsend, rrecv, ssend, srecv,
):
    d = lax.axis_index("dir")
    z = lax.axis_index("region")
    c = lax.rem(d, 2)
    chip = lax.div(d, 2)
    x = lax.rem(chip, 4)
    y = lax.div(chip, 4)
    pa = x + c * (y - x)
    pb = y + c * (x - y)
    oc = 1 - c

    def dev(a, b, zz=None):
        xx = a + c * (b - a)
        yy = b + c * (a - b)
        return ((yy * 4 + xx) * 2 + c, z if zz is None else zz)

    partner = (d + 1 - 2 * c, z)
    a_up, a_dn = dev(m4(pa + 1), pb), dev(m4(pa - 1), pb)
    b_up, b_dn = dev(pa, m4(pb + 1)), dev(pa, m4(pb - 1))
    z_up, z_dn = dev(pa, pb, m4(z + 1)), dev(pa, pb, m4(z - 1))

    barrier = pltpu.get_barrier_semaphore()
    for peer in (z_up, z_dn, a_up, a_dn, b_up, b_dn, partner):
        pl.semaphore_signal(barrier, inc=1, device_id=peer, device_id_type=MESH)

    lane0 = pl.multiple_of(c * 128, 128)
    own_half = cur_in.at[:, :, pl.ds(lane0, 128)]

    def base(oa, ob):
        return (m4(pa - oa) * 4 + m4(pb - ob)) * BLK

    own0 = base(0, 0)
    loads = {}

    def load(name, src_ref, dst_ref):
        loads[name] = pltpu.make_async_copy(src_ref, dst_ref, lsem.at[len(loads)])
        loads[name].start()

    load("keep", own_half, cur.at[pl.ds(own0, 6)])
    load("src", src_in, sraw.at[0])
    load("tid", tid_in, sraw.at[1])
    load("tt", tt_in.at[:, pl.ds(pl.multiple_of(pb * 384, 128), 384)], tts)
    load("rad", rad_in.at[pl.ds(pl.multiple_of((pb * 4 + pa) * TB, 16), TB)], rad)
    load("rcv", rcv_in.at[:, pl.ds(pl.multiple_of(pb * 384, 128), 384)], rcv)
    load("near", near_in, near_v.at[0])
    load("offs", offs_in, offs)

    pl.semaphore_wait(barrier, 7)
    pending = []

    def remote(src_ref, dst_ref, send, recv, to):
        return pltpu.make_async_remote_copy(
            src_ref=src_ref, dst_ref=dst_ref, send_sem=send, recv_sem=recv,
            device_id=to, device_id_type=MESH,
        )

    def go(copy):
        copy.start()
        pending.append(copy)

    def arrived(ref, sem):
        remote(ref, ref, psend.at[0], sem, partner).wait_recv()

    count = [0]

    def send_main(oa, ob, lo, n, to, ra, rb, piece, origin=None):
        part = cur.at[pl.ds(base(oa, ob) + lo, n)]
        go(remote(part if origin is None else origin, part,
                  asend.at[count[0]], arecv.at[(ra * 4 + rb) * 3 + piece], to))
        count[0] += 1

    def got_main(oa, ob, lo, n, piece):
        arrived(cur.at[pl.ds(base(oa, ob) + lo, n)], arecv.at[(oa * 4 + ob) * 3 + piece])

    def z_target(oa, ob):
        a_, b_ = m4(pa - oa), m4(pb - ob)
        yb = b_ + c * (a_ - b_)
        return dev(pa, pb, m4(z + 2 * lax.div(yb, 2) - 1))

    def zb_at(oa, ob):
        a_, b_ = m4(pa - oa), m4(pb - ob)
        return 16 * BLK + ((a_ * 2 + lax.rem(b_, 2)) * 2 + lax.div(b_, 2)) * (12 - RIM)

    def send_zb(oa, ob):
        go(remote(
            cur.at[pl.ds(base(oa, ob) + RIM, 12 - RIM)], cur.at[pl.ds(zb_at(oa, ob), 12 - RIM)],
            zsend.at[oa * 4 + ob], zrecv.at[oa * 4 + ob], z_target(oa, ob),
        ))

    def got_zb(oa, ob):
        arrived(cur.at[pl.ds(zb_at(oa, ob), 12 - RIM)], zrecv.at[oa * 4 + ob])

    def send_own(lo, n, piece, origin=None):
        send_main(0, 0, lo, n, a_up, 1, 0, piece, origin)
        send_main(0, 0, lo, n, a_dn, 3, 0, piece, origin)
        send_main(0, 0, lo, n, b_up, 0, 1, piece, origin)
        send_main(0, 0, lo, n, b_dn, 0, 3, piece, origin)

    go(remote(
        cur_in.at[:, :, pl.ds(pl.multiple_of(oc * 128, 128), 128)],
        cur.at[pl.ds((pb * 4 + pa) * BLK + 6, 6)], psend.at[0], precv.at[0], partner,
    ))
    go(remote(
        cur_in.at[pl.ds(0, RIM), :, pl.ds(lane0, 128)], cur.at[pl.ds(own0 + 12, RIM)],
        zsend.at[16], zrecv.at[16], z_target(0, 0),
    ))
    send_own(0, 6, 0, own_half)
    go(remote(near_in, near_v.at[1], psend.at[1], precv.at[1], partner))
    loads["keep"].wait()
    arrived(cur.at[pl.ds(own0 + 6, 6)], precv.at[0])
    send_own(6, 6, 1)
    send_zb(0, 0)
    arrived(cur.at[pl.ds(own0 + 12, RIM)], zrecv.at[16])
    send_own(12, RIM, 2)
    load("nb", nb_in, nb.at[pl.ds(0, 6)])
    go(remote(nb_in, nb.at[pl.ds(6, 6)], psend.at[2], precv.at[2], partner))
    cur[384] = jnp.zeros((128, 128), BF)

    def slot_of(s, field):
        halo = (s < 96) | (s >= 288)
        i = jnp.where(s < 96, s + 96, jnp.where(s >= 288, s - 288, s - 96))
        box_chip = lax.shift_right_arithmetic(i * 5462, 16)
        p = i - 12 * box_chip - 6 * c
        p = jnp.where(p < 0, p + 12, p)
        by = lax.shift_right_arithmetic(box_chip, 2)
        bx = box_chip - 4 * by
        a = bx + c * (by - bx)
        b = by + c * (bx - by)
        b_hi = lax.shift_right_arithmetic(b, 1)
        size, rim = (BLK, RIM) if field else (16, 4)
        main = (a * 4 + b) * size + p
        beyond = 16 * size + ((a * 2 + b - 2 * b_hi) * 2 + b_hi) * (12 - rim) + (p - rim)
        slot = jnp.where(halo, jnp.where(p < rim, main + 12, beyond), main)
        low = jnp.where(z == 0, 96, 0)
        high = jnp.where(z == 3, 288, 384)
        return jnp.where((s < low) | (s >= high), -1, slot)

    def table(values, ref):
        stage[...] = jnp.full((128, 256), -1.0, F32)
        stage[0:48, 0:192] = values
        stage[64:112, 0:192] = values
        ref[0:128, :] = jnp.transpose(stage[:, 0:128])
        ref[128:256, :] = jnp.transpose(stage[:, 128:256])

    loads["src"].wait()
    table(slot_of(sraw[0], False).astype(F32), src)
    loads["tid"].wait()
    table(sraw[1].astype(F32), tid)
    loads["tt"].wait()
    wide[...] = jnp.zeros((384, 384), F32)
    wide[0:316, :] = tts[...].astype(F32)
    tt_t[...] = jnp.transpose(wide[...]).astype(BF)
    loads["rad"].wait()

    def pattern_block(at, box):
        for i in range(8):
            two = jnp.concatenate([cur[box(2 * i)], cur[box(2 * i + 1)]], axis=1)
            o = jnp.dot(rad[...], two, preferred_element_type=F32)
            bpat[2 * i] = o[:, :128].astype(BF)
            bpat[2 * i + 1] = o[:, 128:].astype(BF)

        def turn(i, _):
            t0 = pl.multiple_of(i * 16, 16)
            pat[pl.ds(t0, 16), pl.ds(at, 16), :] = jnp.swapaxes(bpat[:, pl.ds(t0, 16), :], 0, 1)
            return 0

        lax.fori_loop(0, TB // 16, turn, 0, unroll=2)

    def patterns(*blocks):
        for oa, ob in blocks:
            first = base(oa, ob)
            at = (m4(pa - oa) * 4 + m4(pb - ob)) * 16
            pattern_block(pl.multiple_of(at, 16), lambda i, first=first: first + i)

    def pattern_zb(oa, ob):
        got_zb(oa, ob)
        got_zb(oa, ob + 2)
        a_, parity = m4(pa - oa), lax.rem(m4(pb - ob), 2)
        g = a_ * 2 + parity
        rim0 = (a_ * 4 + parity) * BLK + 16
        over0 = 16 * BLK + g * 2 * (12 - RIM)

        def box(i):
            second, q = i // 8, i % 8
            return rim0 + second * 2 * BLK + q if q < RIM - 4 else over0 + second * (12 - RIM) + q - (RIM - 4)

        pattern_block(pl.multiple_of(256 + g * 16, 16), box)

    n_iota = lax.broadcasted_iota(jnp.int32, (384, 128), 0).astype(F32)
    lane = lax.broadcasted_iota(jnp.int32, (TB, 128), 1)

    def box_row(jp):
        late = jnp.where(jp >= 144, 1, 0)
        at = jp - 144 * late
        size = 36 - 24 * late
        a_ = lax.div(at * (1 + 2 * late), 36)
        rest = at - a_ * size
        which = lax.div(rest, 12)
        p = rest - which * 12
        b_ = m4(pb + jnp.where(late == 1, 0, jnp.where(which == 2, 3, 2 - which)))
        chip_ = (b_ + c * (a_ - b_)) * 4 + a_ + c * (b_ - a_)
        return chip_ * 12 + lax.rem(p + 6 * c, 12)

    def hot(ref, lo, hi):
        row = jnp.where(lane[:1] < 64, ref[pl.ds(lo, 1), :], ref[pl.ds(hi, 1), :])
        return jnp.where(n_iota == row, 1.0, 0.0).astype(BF)

    def mat_group(g):
        def two_rows(it, _):
            rows = [(box_row(g * 16 + 2 * it + p), box_row(g * 16 + 8 + 2 * it + p)) for p in range(2)]
            classes = jnp.concatenate([hot(tid, *rows[0]), hot(tid, *rows[1])], axis=1)
            coef = jnp.dot(
                tt_t[pl.ds(pl.multiple_of(pa * TB, 16), TB), :], classes, preferred_element_type=F32
            )
            for p in range(2):
                part = coef[:, p * 128 : (p + 1) * 128]
                both = jnp.concatenate(
                    [jnp.where(lane < 64, part, 0.0), jnp.where(lane < 64, 0.0, part)], axis=0
                ).astype(BF)
                placed = lax.dot_general(
                    both, hot(src, *rows[p]), (((1,), (1,)), ((), ())), preferred_element_type=F32
                )
                for h in range(2):
                    bmat[h * 8 + 2 * it + p] = placed[h * TB : (h + 1) * TB].astype(BF)
            return 0

        lax.fori_loop(0, 4, two_rows, 0, unroll=4)
        j0 = pl.multiple_of(g * 16, 16)

        def turn(i, _):
            t0 = pl.multiple_of(i * 16, 16)
            for q in range(3):
                lanes = slice(q * 128, (q + 1) * 128)
                mat[pl.ds(t0, 16), pl.ds(j0, 16), lanes] = jnp.swapaxes(bmat[:, pl.ds(t0, 16), lanes], 0, 1)
            return 0

        lax.fori_loop(0, TB // 16, turn, 0)

    def mats(lo, hi):
        lax.fori_loop(lo, hi, lambda g, _: (mat_group(g), 0)[1], 0)

    def line_event(oa):
        send_main(oa, 0, 0, BLK, b_up, oa, 1, 0)
        send_main(oa, 0, 0, BLK, b_dn, oa, 3, 0)

    odd = lax.rem(y, 2)
    line1 = 3 - 2 * c * (1 - odd)
    line2 = 1 + c
    line3 = 2 + c * (1 - 2 * odd)

    def halves(oa, ob):
        got_main(oa, ob, 0, HALF, 0)
        got_main(oa, ob, HALF, BLK - HALF, 1)
        send_zb(oa, ob)

    def ring_event(oa):
        for ob, lo, n, to, piece in ((1, 0, HALF, b_up, 0), (3, HALF, BLK - HALF, b_dn, 1)):
            got_main(oa, ob, 0, BLK, 0)
            send_main(oa, ob, lo, n, to, oa, 2, piece)
            send_zb(oa, ob)

    for oa, ob in ((1, 0), (3, 0), (0, 1), (0, 3)):
        got_main(oa, ob, 0, 6, 0)
        got_main(oa, ob, 6, 6, 1)
        if (oa, ob) == (1, 0):
            send_main(1, 0, 0, HALF, a_up, 2, 0, 0)
        if (oa, ob) == (0, 1):
            send_main(0, 1, 0, HALF, b_up, 0, 2, 0)
        send_zb(oa, ob)
    got_main(3, 0, 12, RIM, 2)
    send_main(3, 0, HALF, BLK - HALF, a_dn, 2, 0, 1)
    got_main(1, 0, 12, RIM, 2)
    line_event(line1)
    got_main(0, 3, 12, RIM, 2)
    send_main(0, 3, HALF, BLK - HALF, b_dn, 0, 2, 1)
    got_main(0, 1, 12, RIM, 2)
    mats(0, 1)
    patterns((0, 0))
    halves(2, 0)
    line_event(line2)
    mats(1, 2)
    patterns((1, 0))
    ring_event(line1)
    line_event(line3)
    mats(2, 3)
    patterns((3, 0), (2, 0))
    halves(0, 2)
    mats(3, 5)
    patterns((0, 1), (0, 3))
    ring_event(line2)
    mats(5, 7)
    patterns((line1, 1), (line1, 3), (0, 2))
    halves(line1, 2)
    mats(7, 9)
    patterns((line2, 1), (line2, 3))
    ring_event(line3)
    mats(9, 12)
    halves(line2, 2)
    patterns((line3, 1), (line3, 3), (line1, 2), (line2, 2))
    halves(line3, 2)
    patterns((line3, 2))
    for oa, ob in (
        (0, 0), (0, 1), (line1, 1), (line1, 0), (line2, 1), (line2, 0), (line3, 1), (line3, 0)
    ):
        pattern_zb(oa, ob)

    first_row, rows_of = (0, 144), (36, 12)
    own_copies = []

    def chunk(h, k):
        n = h * 3 + k
        j0, n_rows = first_row[h], rows_of[h]
        n_half, n_tiles = n_rows // 2, n_rows // 4

        def one(i, _):
            t = k * TCH + i
            o = jnp.dot(mat[t, j0 : j0 + 4 * n_rows, :], pat[t], preferred_element_type=F32)
            btr[i, 0 : 4 * n_rows] = o.astype(BF)
            return 0

        lax.fori_loop(0, TCH, one, 0, unroll=8)

        def pack(i, _):
            r0 = pl.multiple_of(lax.rem(i, n_tiles) * 16, 16)
            t0 = pl.multiple_of(lax.div(i, n_tiles) * 16, 16)
            tx[pl.ds(j0 + r0, 16), pl.ds(k * TCH + t0, 16), :] = jnp.swapaxes(
                btr[pl.ds(t0, 16), pl.ds(r0, 16), :], 0, 1
            )
            return 0

        lax.fori_loop(0, 2 * n_tiles, pack, 0, unroll=2)
        ts = pl.ds(k * TCH, TCH)
        here = pl.ds(h * 36, n_rows)
        there = rx_at(pa, k)
        far = j0 + m4(pa + 2) * n_rows
        hop_rows = pl.ds(0, n_half)
        go(remote(tx.at[pl.ds(far, n_half), ts], relay.at[0, n, hop_rows], rsend.at[n * 6 + 2], rrecv.at[n * 6 + 2], a_up))
        go(remote(tx.at[pl.ds(far + n_half, n_half), ts], relay.at[1, n, hop_rows], rsend.at[n * 6 + 3], rrecv.at[n * 6 + 3], a_dn))
        go(remote(tx.at[pl.ds(j0 + m4(pa + 1) * n_rows, n_rows), ts], rx.at[here, there], rsend.at[n * 6], rrecv.at[n * 6], a_up))
        go(remote(tx.at[pl.ds(j0 + m4(pa - 1) * n_rows, n_rows), ts], rx.at[here, there], rsend.at[n * 6 + 1], rrecv.at[n * 6 + 1], a_dn))
        own = pltpu.make_async_copy(tx.at[pl.ds(j0 + pa * n_rows, n_rows), ts], rx.at[here, there], lsem.at[10 + n])
        own.start()
        own_copies.append(own)

    def rx_at(a_, k):
        return pl.ds(pl.multiple_of(a_ * TB + k * TCH, TCH), TCH)

    def forward(h, k):
        n = h * 3 + k
        n_half = rows_of[h] // 2
        for way, o, to in ((0, -1, a_up), (1, 1, a_dn)):
            held = relay.at[way, n, pl.ds(0, n_half)]
            arrived(held, rrecv.at[n * 6 + 2 + way])
            go(remote(held, rx.at[pl.ds(h * 36 + way * n_half, n_half), rx_at(m4(pa + o), k)],
                      rsend.at[n * 6 + 4 + way], rrecv.at[n * 6 + 4 + way], to))

    def all_here(h):
        n_half = rows_of[h] // 2
        here = pl.ds(h * 36, 2 * n_half)
        for k in range(3):
            n = h * 3 + k
            own_copies[n].wait()
            arrived(rx.at[here, rx_at(m4(pa - 1), k)], rrecv.at[n * 6])
            arrived(rx.at[here, rx_at(m4(pa + 1), k)], rrecv.at[n * 6 + 1])
            for way in range(2):
                arrived(rx.at[pl.ds(h * 36 + way * n_half, n_half), rx_at(m4(pa + 2), k)],
                        rrecv.at[n * 6 + 4 + way])

    def near_boxes(which, lo, hi):
        def box(i, _):
            w = which * 6 + i
            total = jnp.zeros((128, 128), F32)
            for m in range(0, 26, 2):
                blocks = jnp.concatenate([nb[w, m], nb[w, m + 1]], axis=1)
                fields = jnp.concatenate([cur[ns[which, i, 0, m]], cur[ns[which, i, 0, m + 1]]], axis=0)
                total += jnp.dot(blocks, fields, preferred_element_type=F32)
            total += jnp.dot(nb[w, 26], cur[ns[which, i, 0, 26]], preferred_element_type=F32)
            acc[w] = total
            return 0

        lax.fori_loop(lo, hi, box, 0)

    def contract(group, put):
        def pair(i, _):
            j = group * 12 + 2 * i
            two = jnp.concatenate([rx[j], rx[j + 1]], axis=1)
            o = jnp.dot(rw[...], two, preferred_element_type=F32)
            put(2 * i, o[:, :128])
            put(2 * i + 1, o[:, 128:])
            return 0

        lax.fori_loop(0, 6, pair, 0)

    def partial_to(group, o, to):
        def put(w, v):
            ps[o - 1, w] = v.astype(BF)

        contract(group, put)
        go(remote(ps.at[o - 1], pr.at[o - 1], ssend.at[o - 1], srecv.at[o - 1], to))

    def put_acc(w, v):
        acc[w] = acc[w] + v

    chunk(0, 0)
    chunk(0, 1)
    forward(0, 0)
    chunk(0, 2)
    loads["rcv"].wait()
    loads["offs"].wait()
    k_at = lax.broadcasted_iota(jnp.int32, (8, 384), 1) + pb * 384
    width = jnp.zeros((8, 384), jnp.int32)
    for i in range(32):
        lo, hi = offs[i], offs[i + 1]
        width = jnp.where((k_at >= lo) & (k_at < hi), hi - lo, width)
    weight = 1536.0 / (32.0 * width.astype(F32))
    rw[...] = (rcv[...].astype(F32) * weight[:1]).astype(BF)
    loads["near"].wait()
    arrived(near_v.at[1], precv.at[1])
    near_s = near_v[...]
    near_s = slot_of(jnp.where(near_s < 0, -1, near_s + 48), True)
    near_m[...] = jnp.where(near_s < 0, 384, near_s)
    forward(0, 1)
    load("ns", near_m, ns)
    chunk(1, 0)
    chunk(1, 1)
    forward(0, 2)
    chunk(1, 2)
    loads["ns"].wait()
    loads["nb"].wait()
    near_boxes(0, 0, 4)
    forward(1, 0)
    all_here(0)

    def put_far(w, v):
        ps[1, w] = v.astype(BF)

    contract(0, put_far)
    go(remote(ps.at[1, pl.ds(0, 6)], hop.at[0], ssend.at[1], srecv.at[1], b_up))
    go(remote(ps.at[1, pl.ds(6, 6)], hop.at[1], ssend.at[3], srecv.at[3], b_dn))
    partial_to(1, 1, b_up)
    partial_to(2, 3, b_dn)
    forward(1, 1)
    arrived(hop.at[0], srecv.at[1])
    go(remote(hop.at[0], pr.at[1, pl.ds(0, 6)], ssend.at[4], srecv.at[4], b_up))
    arrived(hop.at[1], srecv.at[3])
    go(remote(hop.at[1], pr.at[1, pl.ds(6, 6)], ssend.at[5], srecv.at[5], b_dn))
    forward(1, 2)
    near_boxes(0, 4, 6)
    arrived(nb.at[pl.ds(6, 6)], precv.at[2])
    near_boxes(1, 0, 6)
    all_here(1)
    contract(3, put_acc)
    arrived(pr.at[0], srecv.at[0])
    arrived(pr.at[2], srecv.at[2])
    arrived(pr.at[1, pl.ds(0, 6)], srecv.at[4])
    arrived(pr.at[1, pl.ds(6, 6)], srecv.at[5])

    def finish(which):
        def one(i, _):
            w = which * 6 + i
            total = acc[w] + pr[0, w].astype(F32) + pr[1, w].astype(F32) + pr[2, w].astype(F32)
            fin[which, i] = total.astype(BF)
            return 0

        lax.fori_loop(0, 6, one, 0)

    mine = pl.ds(lane0, 128)
    theirs = pl.ds(pl.multiple_of(oc * 128, 128), 128)
    finish(1)
    go(remote(fin.at[1], out.at[:, :, mine], psend.at[3], precv.at[3], partner))
    finish(0)
    write = pltpu.make_async_copy(fin.at[0], out.at[:, :, mine], lsem.at[16])
    write.start()
    write.wait()
    arrived(out.at[:, :, theirs], precv.at[3])
    for copy in pending:
        copy.wait_send()


def shards(currents, radiate, receive, transfer_table, near_blocks, dir_offsets, trans_src, trans_tid, near_src):
    any_spec = pl.BlockSpec(memory_space=pl.ANY)
    dma = pltpu.SemaphoreType.DMA
    out = pl.pallas_call(
        body,
        out_shape=jax.ShapeDtypeStruct((6, 128, 256), BF),
        in_specs=[any_spec] * 9,
        out_specs=any_spec,
        scratch_shapes=[
            pltpu.VMEM((385, 128, 128), BF),
            pltpu.VMEM((12, 27, 128, 128), BF),
            pltpu.VMEM((TB, 192, 384), BF),
            pltpu.VMEM((TB, 384, 128), BF),
            pltpu.VMEM((192, TB, 128), BF),
            pltpu.VMEM((48, 4 * TB, 128), BF),
            pltpu.VMEM((2, NCH, 18, TCH, 128), BF),
            pltpu.VMEM((2, 6, 128, 128), BF),
            pltpu.VMEM((3, 12, 128, 128), BF),
            pltpu.VMEM((3, 12, 128, 128), BF),
            pltpu.VMEM((12, 128, 128), F32),
            pltpu.VMEM((16, TB, 128), BF),
            pltpu.VMEM((16, TB, 384), BF),
            pltpu.VMEM((TCH, 144, 128), BF),
            pltpu.VMEM((TB, 128), BF),
            pltpu.VMEM((128, 384), BF),
            pltpu.VMEM((128, 384), BF),
            pltpu.VMEM((2, 6, 128, 128), BF),
            pltpu.VMEM((2, 6, 1, 27), jnp.int32),
            pltpu.VMEM((2, 6, 1, 27), jnp.int32),
            pltpu.SMEM((2, 6, 1, 27), jnp.int32),
            pltpu.VMEM((316, 384), BF),
            pltpu.VMEM((384, 384), F32),
            pltpu.VMEM((384, 384), BF),
            pltpu.VMEM((2, 48, 192), jnp.int32),
            pltpu.VMEM((128, 256), F32),
            pltpu.VMEM((256, 128), F32),
            pltpu.VMEM((256, 128), F32),
            pltpu.SMEM((33,), jnp.int32),
            dma((17,)),
            dma((4,)),
            dma((4,)),
            dma((48,)),
            dma((48,)),
            dma((17,)),
            dma((17,)),
            dma((36,)),
            dma((36,)),
            dma((6,)),
            dma((6,)),
        ],
        compiler_params=pltpu.CompilerParams(
            collective_id=0, has_side_effects=True, vmem_limit_bytes=67043328
        ),
        name="fmm",
    )(
        currents[0], radiate, receive, near_blocks[0], jnp.swapaxes(near_src, 0, 1), transfer_table,
        jnp.swapaxes(trans_src[0], 0, 1), jnp.swapaxes(trans_tid[0], 0, 1), dir_offsets,
    )
    return out[None]


def solution(mesh):
    placed = (
        P("region", "dir", None, None),
        P(),
        P(),
        P(),
        P("region", "dir", None, None, None),
        P(),
        P("region", None, None),
        P("region", None, None),
        P("region", "dir", None),
    )
    return jax.shard_map(
        shards,
        mesh=mesh,
        in_specs=placed,
        out_specs=P("region", "dir", None, None),
        check_vma=False,
    )
```

```python
import jax
import jax.numpy as jnp
from jax import lax
from jax.experimental import pallas as pl
from jax.experimental.pallas import tpu as pltpu
from jax.sharding import PartitionSpec as P

MESH = pl.DeviceIdType.MESH
BF = jnp.bfloat16
F32 = jnp.float32
TB = 96
CHUNKS = ((0, 0, 16), (0, 16, 32), (0, 48, 32), (0, 80, 16), (1, 0, 32), (1, 32, 32), (1, 64, 32))
RIM = 6
BLK = 12 + RIM
HALF = (BLK + 1) // 2


def m4(v):
    return lax.rem(v + 8, 4)


def body(
    cur_in, rad_in, rcv_in, nb_in, near_in, tt_in, src_in, tid_in, offs_in, out,
    cur, nb, mat, pat, tx, rx, relay, relay2, hop, ps, pr, acc, bpat, bmat, btr, rad, rcv, rw, fin,
    near_v, near_m, ns, tts, wide, tt_t, sraw, stage, src, tid, offs,
    lsem, psend, precv, asend, arecv, zsend, zrecv, rsend, rrecv, ssend, srecv,
):
    d = lax.axis_index("dir")
    z = lax.axis_index("region")
    c = lax.rem(d, 2)
    chip = lax.div(d, 2)
    x = lax.rem(chip, 4)
    y = lax.div(chip, 4)
    pa = x + c * (y - x)
    pb = y + c * (x - y)
    oc = 1 - c

    def dev(a, b, zz=None):
        xx = a + c * (b - a)
        yy = b + c * (a - b)
        return ((yy * 4 + xx) * 2 + c, z if zz is None else zz)

    partner = (d + 1 - 2 * c, z)
    a_up, a_dn = dev(m4(pa + 1), pb), dev(m4(pa - 1), pb)
    b_up, b_dn = dev(pa, m4(pb + 1)), dev(pa, m4(pb - 1))
    z_up, z_dn = dev(pa, pb, m4(z + 1)), dev(pa, pb, m4(z - 1))

    barrier = pltpu.get_barrier_semaphore()
    for peer in (z_up, z_dn, a_up, a_dn, b_up, b_dn, partner):
        pl.semaphore_signal(barrier, inc=1, device_id=peer, device_id_type=MESH)

    lane0 = pl.multiple_of(c * 128, 128)
    own_half = cur_in.at[:, :, pl.ds(lane0, 128)]

    def base(oa, ob):
        return (m4(pa - oa) * 4 + m4(pb - ob)) * BLK

    own0 = base(0, 0)
    loads = {}

    def load(name, src_ref, dst_ref):
        loads[name] = pltpu.make_async_copy(src_ref, dst_ref, lsem.at[len(loads)])
        loads[name].start()

    load("keep", own_half, cur.at[pl.ds(own0, 6)])
    load("src", src_in, sraw.at[0])
    load("tid", tid_in, sraw.at[1])
    load("tt", tt_in.at[:, pl.ds(pl.multiple_of(pb * 384, 128), 384)], tts)
    load("rad", rad_in.at[pl.ds(pl.multiple_of((pb * 4 + pa) * TB, 16), TB)], rad)
    load("rcv", rcv_in.at[:, pl.ds(pl.multiple_of(pb * 384, 128), 384)], rcv)
    load("near", near_in, near_v.at[0])
    load("offs", offs_in, offs)

    pl.semaphore_wait(barrier, 7)
    pending = []

    def remote(src_ref, dst_ref, send, recv, to):
        return pltpu.make_async_remote_copy(
            src_ref=src_ref, dst_ref=dst_ref, send_sem=send, recv_sem=recv,
            device_id=to, device_id_type=MESH,
        )

    def go(copy):
        copy.start()
        pending.append(copy)

    def arrived(ref, sem):
        remote(ref, ref, psend.at[0], sem, partner).wait_recv()

    count = [0]

    def send_main(oa, ob, lo, n, to, ra, rb, piece, origin=None):
        part = cur.at[pl.ds(base(oa, ob) + lo, n)]
        go(remote(part if origin is None else origin, part,
                  asend.at[count[0]], arecv.at[(ra * 4 + rb) * 3 + piece], to))
        count[0] += 1

    def got_main(oa, ob, lo, n, piece):
        arrived(cur.at[pl.ds(base(oa, ob) + lo, n)], arecv.at[(oa * 4 + ob) * 3 + piece])

    def z_target(oa, ob):
        a_, b_ = m4(pa - oa), m4(pb - ob)
        yb = b_ + c * (a_ - b_)
        return dev(pa, pb, m4(z + 2 * lax.div(yb, 2) - 1))

    def zb_at(oa, ob):
        a_, b_ = m4(pa - oa), m4(pb - ob)
        return 16 * BLK + ((a_ * 2 + lax.rem(b_, 2)) * 2 + lax.div(b_, 2)) * (12 - RIM)

    def send_zb(oa, ob):
        go(remote(
            cur.at[pl.ds(base(oa, ob) + RIM, 12 - RIM)], cur.at[pl.ds(zb_at(oa, ob), 12 - RIM)],
            zsend.at[oa * 4 + ob], zrecv.at[oa * 4 + ob], z_target(oa, ob),
        ))

    def got_zb(oa, ob):
        arrived(cur.at[pl.ds(zb_at(oa, ob), 12 - RIM)], zrecv.at[oa * 4 + ob])

    def send_own(lo, n, piece, origin=None):
        send_main(0, 0, lo, n, a_up, 1, 0, piece, origin)
        send_main(0, 0, lo, n, a_dn, 3, 0, piece, origin)
        send_main(0, 0, lo, n, b_up, 0, 1, piece, origin)
        send_main(0, 0, lo, n, b_dn, 0, 3, piece, origin)

    go(remote(
        cur_in.at[:, :, pl.ds(pl.multiple_of(oc * 128, 128), 128)],
        cur.at[pl.ds((pb * 4 + pa) * BLK + 6, 6)], psend.at[0], precv.at[0], partner,
    ))
    go(remote(
        cur_in.at[pl.ds(0, RIM), :, pl.ds(lane0, 128)], cur.at[pl.ds(own0 + 12, RIM)],
        zsend.at[16], zrecv.at[16], z_target(0, 0),
    ))
    send_own(0, 6, 0, own_half)
    go(remote(near_in, near_v.at[1], psend.at[1], precv.at[1], partner))
    loads["keep"].wait()
    arrived(cur.at[pl.ds(own0 + 6, 6)], precv.at[0])
    send_own(6, 6, 1)
    send_zb(0, 0)
    arrived(cur.at[pl.ds(own0 + 12, RIM)], zrecv.at[16])
    send_own(12, RIM, 2)
    load("nb", nb_in, nb.at[pl.ds(0, 6)])
    go(remote(nb_in, nb.at[pl.ds(6, 6)], psend.at[2], precv.at[2], partner))
    cur[384] = jnp.zeros((128, 128), BF)

    def slot_of(s, field):
        halo = (s < 96) | (s >= 288)
        i = jnp.where(s < 96, s + 96, jnp.where(s >= 288, s - 288, s - 96))
        box_chip = lax.shift_right_arithmetic(i * 5462, 16)
        p = i - 12 * box_chip - 6 * c
        p = jnp.where(p < 0, p + 12, p)
        by = lax.shift_right_arithmetic(box_chip, 2)
        bx = box_chip - 4 * by
        a = bx + c * (by - bx)
        b = by + c * (bx - by)
        b_hi = lax.shift_right_arithmetic(b, 1)
        size, rim = (BLK, RIM) if field else (16, 4)
        main = (a * 4 + b) * size + p
        beyond = 16 * size + ((a * 2 + b - 2 * b_hi) * 2 + b_hi) * (12 - rim) + (p - rim)
        slot = jnp.where(halo, jnp.where(p < rim, main + 12, beyond), main)
        low = jnp.where(z == 0, 96, 0)
        high = jnp.where(z == 3, 288, 384)
        return jnp.where((s < low) | (s >= high), -1, slot)

    def table(values, ref):
        stage[...] = jnp.full((128, 256), -1.0, F32)
        stage[0:48, 0:192] = values
        stage[64:112, 0:192] = values
        ref[0:128, :] = jnp.transpose(stage[:, 0:128])
        ref[128:256, :] = jnp.transpose(stage[:, 128:256])

    loads["src"].wait()
    table(slot_of(sraw[0], False).astype(F32), src)
    loads["tid"].wait()
    table(sraw[1].astype(F32), tid)
    loads["tt"].wait()
    wide[...] = jnp.zeros((384, 384), F32)
    wide[0:316, :] = tts[...].astype(F32)
    tt_t[...] = jnp.transpose(wide[...]).astype(BF)
    loads["rad"].wait()

    def pattern_block(at, box):
        for i in range(8):
            two = jnp.concatenate([cur[box(2 * i)], cur[box(2 * i + 1)]], axis=1)
            o = jnp.dot(rad[...], two, preferred_element_type=F32)
            bpat[2 * i] = o[:, :128].astype(BF)
            bpat[2 * i + 1] = o[:, 128:].astype(BF)

        def turn(i, _):
            t0 = pl.multiple_of(i * 16, 16)
            pat[pl.ds(t0, 16), pl.ds(at, 16), :] = jnp.swapaxes(bpat[:, pl.ds(t0, 16), :], 0, 1)
            return 0

        lax.fori_loop(0, TB // 16, turn, 0, unroll=2)

    def patterns(*blocks):
        for oa, ob in blocks:
            first = base(oa, ob)
            at = (m4(pa - oa) * 4 + m4(pb - ob)) * 16
            pattern_block(pl.multiple_of(at, 16), lambda i, first=first: first + i)

    def pattern_zb(oa, ob):
        got_zb(oa, ob)
        got_zb(oa, ob + 2)
        a_, parity = m4(pa - oa), lax.rem(m4(pb - ob), 2)
        g = a_ * 2 + parity
        rim0 = (a_ * 4 + parity) * BLK + 16
        over0 = 16 * BLK + g * 2 * (12 - RIM)

        def box(i):
            second, q = i // 8, i % 8
            return rim0 + second * 2 * BLK + q if q < RIM - 4 else over0 + second * (12 - RIM) + q - (RIM - 4)

        pattern_block(pl.multiple_of(256 + g * 16, 16), box)

    n_iota = lax.broadcasted_iota(jnp.int32, (384, 128), 0).astype(F32)
    lane = lax.broadcasted_iota(jnp.int32, (TB, 128), 1)

    def box_row(jp):
        late = jnp.where(jp >= 144, 1, 0)
        at = jp - 144 * late
        size = 36 - 24 * late
        a_ = lax.div(at * (1 + 2 * late), 36)
        rest = at - a_ * size
        which = lax.div(rest, 12)
        p = rest - which * 12
        b_ = m4(pb + jnp.where(late == 1, 0, jnp.where(which == 2, 3, 2 - which)))
        chip_ = (b_ + c * (a_ - b_)) * 4 + a_ + c * (b_ - a_)
        return chip_ * 12 + lax.rem(p + 6 * c, 12)

    def hot(ref, lo, hi):
        row = jnp.where(lane[:1] < 64, ref[pl.ds(lo, 1), :], ref[pl.ds(hi, 1), :])
        return jnp.where(n_iota == row, 1.0, 0.0).astype(BF)

    def mat_group(g):
        def two_rows(it, _):
            rows = [(box_row(g * 16 + 2 * it + p), box_row(g * 16 + 8 + 2 * it + p)) for p in range(2)]
            classes = jnp.concatenate([hot(tid, *rows[0]), hot(tid, *rows[1])], axis=1)
            coef = jnp.dot(
                tt_t[pl.ds(pl.multiple_of(pa * TB, 16), TB), :], classes, preferred_element_type=F32
            )
            for p in range(2):
                part = coef[:, p * 128 : (p + 1) * 128]
                both = jnp.concatenate(
                    [jnp.where(lane < 64, part, 0.0), jnp.where(lane < 64, 0.0, part)], axis=0
                ).astype(BF)
                placed = lax.dot_general(
                    both, hot(src, *rows[p]), (((1,), (1,)), ((), ())), preferred_element_type=F32
                )
                for h in range(2):
                    bmat[h * 8 + 2 * it + p] = placed[h * TB : (h + 1) * TB].astype(BF)
            return 0

        lax.fori_loop(0, 4, two_rows, 0, unroll=4)
        j0 = pl.multiple_of(g * 16, 16)

        def turn(i, _):
            t0 = pl.multiple_of(i * 16, 16)
            for q in range(3):
                lanes = slice(q * 128, (q + 1) * 128)
                mat[pl.ds(t0, 16), pl.ds(j0, 16), lanes] = jnp.swapaxes(bmat[:, pl.ds(t0, 16), lanes], 0, 1)
            return 0

        lax.fori_loop(0, TB // 16, turn, 0)

    def mats(lo, hi):
        lax.fori_loop(lo, hi, lambda g, _: (mat_group(g), 0)[1], 0)

    def line_event(oa):
        send_main(oa, 0, 0, BLK, b_up, oa, 1, 0)
        send_main(oa, 0, 0, BLK, b_dn, oa, 3, 0)

    odd = lax.rem(y, 2)
    line1 = 3 - 2 * c * (1 - odd)
    line2 = 1 + c
    line3 = 2 + c * (1 - 2 * odd)

    def halves(oa, ob):
        got_main(oa, ob, 0, HALF, 0)
        got_main(oa, ob, HALF, BLK - HALF, 1)
        send_zb(oa, ob)

    def ring_event(oa):
        for ob, lo, n, to, piece in ((1, 0, HALF, b_up, 0), (3, HALF, BLK - HALF, b_dn, 1)):
            got_main(oa, ob, 0, BLK, 0)
            send_main(oa, ob, lo, n, to, oa, 2, piece)
            send_zb(oa, ob)

    for oa, ob in ((1, 0), (3, 0), (0, 1), (0, 3)):
        got_main(oa, ob, 0, 6, 0)
        got_main(oa, ob, 6, 6, 1)
        if (oa, ob) == (1, 0):
            send_main(1, 0, 0, HALF, a_up, 2, 0, 0)
        if (oa, ob) == (0, 1):
            send_main(0, 1, 0, HALF, b_up, 0, 2, 0)
        send_zb(oa, ob)
    got_main(3, 0, 12, RIM, 2)
    send_main(3, 0, HALF, BLK - HALF, a_dn, 2, 0, 1)
    got_main(1, 0, 12, RIM, 2)
    line_event(line1)
    got_main(0, 3, 12, RIM, 2)
    send_main(0, 3, HALF, BLK - HALF, b_dn, 0, 2, 1)
    got_main(0, 1, 12, RIM, 2)
    mats(0, 1)
    patterns((0, 0))
    halves(2, 0)
    line_event(line2)
    mats(1, 2)
    patterns((1, 0))
    ring_event(line1)
    line_event(line3)
    mats(2, 3)
    patterns((3, 0), (2, 0))
    halves(0, 2)
    mats(3, 5)
    patterns((0, 1), (0, 3))
    ring_event(line2)
    mats(5, 7)
    patterns((line1, 1), (line1, 3), (0, 2))
    halves(line1, 2)
    mats(7, 9)
    patterns((line2, 1), (line2, 3))
    ring_event(line3)
    mats(9, 12)
    halves(line2, 2)
    patterns((line3, 1), (line3, 3), (line1, 2), (line2, 2))
    halves(line3, 2)
    patterns((line3, 2))
    for oa, ob in (
        (0, 0), (0, 1), (line1, 1), (line1, 0), (line2, 1), (line2, 0), (line3, 1), (line3, 0)
    ):
        pattern_zb(oa, ob)

    first_row, rows_of = (0, 144), (36, 12)
    own_copies = []

    def chunk(n):
        h, t_first, n_dirs = CHUNKS[n]
        j0, n_rows = first_row[h], rows_of[h]
        n_half, n_tiles = n_rows // 2, n_rows // 4

        def one(i, _):
            t = t_first + i
            o = jnp.dot(mat[t, j0 : j0 + 4 * n_rows, :], pat[t], preferred_element_type=F32)
            btr[i, 0 : 4 * n_rows] = o.astype(BF)
            return 0

        lax.fori_loop(0, n_dirs, one, 0, unroll=8)

        def pack(i, _):
            r0 = pl.multiple_of(lax.rem(i, n_tiles) * 16, 16)
            t0 = pl.multiple_of(lax.div(i, n_tiles) * 16, 16)
            tx[pl.ds(j0 + r0, 16), pl.ds(t_first + t0, 16), :] = jnp.swapaxes(
                btr[pl.ds(t0, 16), pl.ds(r0, 16), :], 0, 1
            )
            return 0

        lax.fori_loop(0, n_tiles * n_dirs // 16, pack, 0, unroll=3)
        ts = pl.ds(t_first, n_dirs)
        here = pl.ds(h * 36, n_rows)
        there = rx_at(pa, n)
        far = j0 + m4(pa + 2) * n_rows
        for way, to in ((0, a_up), (1, a_dn)):
            go(remote(tx.at[pl.ds(far + way * n_half, n_half), ts], held(way, n),
                      rsend.at[n * 6 + 2 + way], rrecv.at[n * 6 + 2 + way], to))
        for way, o, to in ((0, 1, a_up), (1, -1, a_dn)):
            go(remote(tx.at[pl.ds(j0 + m4(pa + o) * n_rows, n_rows), ts], rx.at[here, there],
                      rsend.at[n * 6 + way], rrecv.at[n * 6 + way], to))
        own = pltpu.make_async_copy(tx.at[pl.ds(j0 + pa * n_rows, n_rows), ts], rx.at[here, there], lsem.at[10 + n])
        own.start()
        own_copies.append(own)

    def rx_at(a_, n):
        _, t_first, n_dirs = CHUNKS[n]
        return pl.ds(pl.multiple_of(a_ * TB + t_first, 16), n_dirs)

    def held(way, n):
        h, _, n_dirs = CHUNKS[n]
        return relay.at[way, n, :, pl.ds(0, n_dirs)] if h == 0 else relay2.at[way, n - 4]

    def forward(n):
        h = CHUNKS[n][0]
        n_half = rows_of[h] // 2
        for way, o, to in ((0, -1, a_up), (1, 1, a_dn)):
            arrived(held(way, n), rrecv.at[n * 6 + 2 + way])
            go(remote(held(way, n), rx.at[pl.ds(h * 36 + way * n_half, n_half), rx_at(m4(pa + o), n)],
                      rsend.at[n * 6 + 4 + way], rrecv.at[n * 6 + 4 + way], to))

    def all_here(h):
        n_half = rows_of[h] // 2
        here = pl.ds(h * 36, 2 * n_half)
        for n in range(len(CHUNKS)):
            if CHUNKS[n][0] != h:
                continue
            own_copies[n].wait()
            arrived(rx.at[here, rx_at(m4(pa - 1), n)], rrecv.at[n * 6])
            arrived(rx.at[here, rx_at(m4(pa + 1), n)], rrecv.at[n * 6 + 1])
            for way in range(2):
                arrived(rx.at[pl.ds(h * 36 + way * n_half, n_half), rx_at(m4(pa + 2), n)],
                        rrecv.at[n * 6 + 4 + way])

    def near_boxes(which, lo, hi):
        def box(i, _):
            w = which * 6 + i
            total = jnp.zeros((128, 128), F32)
            for m in range(0, 26, 2):
                blocks = jnp.concatenate([nb[w, m], nb[w, m + 1]], axis=1)
                fields = jnp.concatenate([cur[ns[which, i, 0, m]], cur[ns[which, i, 0, m + 1]]], axis=0)
                total += jnp.dot(blocks, fields, preferred_element_type=F32)
            total += jnp.dot(nb[w, 26], cur[ns[which, i, 0, 26]], preferred_element_type=F32)
            acc[w] = total
            return 0

        lax.fori_loop(lo, hi, box, 0)

    def contract(group, put):
        def pair(i, _):
            j = group * 12 + 2 * i
            two = jnp.concatenate([rx[j], rx[j + 1]], axis=1)
            o = jnp.dot(rw[...], two, preferred_element_type=F32)
            put(2 * i, o[:, :128])
            put(2 * i + 1, o[:, 128:])
            return 0

        lax.fori_loop(0, 6, pair, 0)

    def put_acc(w, v):
        acc[w] = acc[w] + v

    chunk(0)
    chunk(1)
    forward(0)
    chunk(2)
    loads["rcv"].wait()
    loads["offs"].wait()
    k_at = lax.broadcasted_iota(jnp.int32, (8, 384), 1) + pb * 384
    width = jnp.zeros((8, 384), jnp.int32)
    for i in range(32):
        lo, hi = offs[i], offs[i + 1]
        width = jnp.where((k_at >= lo) & (k_at < hi), hi - lo, width)
    weight = 1536.0 / (32.0 * width.astype(F32))
    rw[...] = (rcv[...].astype(F32) * weight[:1]).astype(BF)
    loads["near"].wait()
    arrived(near_v.at[1], precv.at[1])
    near_s = near_v[...]
    near_s = slot_of(jnp.where(near_s < 0, -1, near_s + 48), True)
    near_m[...] = jnp.where(near_s < 0, 384, near_s)
    forward(1)
    load("ns", near_m, ns)
    chunk(3)
    chunk(4)
    forward(2)
    chunk(5)
    chunk(6)
    loads["ns"].wait()
    loads["nb"].wait()
    near_boxes(0, 0, 1)
    forward(3)
    near_boxes(0, 1, 4)
    forward(4)
    all_here(0)

    def put_ps(slot):
        def put(w, v):
            ps[slot, w] = v.astype(BF)

        return put

    contract(0, put_ps(2))
    go(remote(ps.at[2, pl.ds(0, 6)], hop.at[0], ssend.at[0], srecv.at[0], b_up))
    go(remote(ps.at[2, pl.ds(6, 6)], hop.at[1], ssend.at[1], srecv.at[1], b_dn))
    contract(1, put_ps(0))
    go(remote(ps.at[0, pl.ds(6, 6)], pr.at[0, pl.ds(6, 6)], ssend.at[2], srecv.at[2], b_up))
    contract(2, put_ps(1))
    go(remote(ps.at[1, pl.ds(0, 6)], pr.at[1, pl.ds(0, 6)], ssend.at[3], srecv.at[3], b_dn))
    forward(5)
    forward(6)
    near_boxes(0, 4, 6)
    for way, to in ((0, b_up), (1, b_dn)):
        arrived(hop.at[way], srecv.at[way])

        def join(i, _, way=way):
            w = way * 6 + i
            ps[way, w] = (ps[way, w].astype(F32) + hop[way, i].astype(F32)).astype(BF)
            return 0

        lax.fori_loop(0, 6, join, 0)
        part = pl.ds(way * 6, 6)
        go(remote(ps.at[way, part], pr.at[way, part], ssend.at[4 + way], srecv.at[4 + way], to))
    arrived(nb.at[pl.ds(6, 6)], precv.at[2])
    near_boxes(1, 0, 6)
    all_here(1)
    contract(3, put_acc)
    arrived(pr.at[0, pl.ds(6, 6)], srecv.at[2])
    arrived(pr.at[1, pl.ds(0, 6)], srecv.at[3])
    arrived(pr.at[0, pl.ds(0, 6)], srecv.at[4])
    arrived(pr.at[1, pl.ds(6, 6)], srecv.at[5])

    def finish(which):
        def one(i, _):
            w = which * 6 + i
            total = acc[w] + pr[0, w].astype(F32) + pr[1, w].astype(F32)
            fin[which, i] = total.astype(BF)
            return 0

        lax.fori_loop(0, 6, one, 0)

    mine = pl.ds(lane0, 128)
    theirs = pl.ds(pl.multiple_of(oc * 128, 128), 128)
    finish(1)
    go(remote(fin.at[1], out.at[:, :, mine], psend.at[3], precv.at[3], partner))
    finish(0)
    write = pltpu.make_async_copy(fin.at[0], out.at[:, :, mine], lsem.at[17])
    write.start()
    write.wait()
    arrived(out.at[:, :, theirs], precv.at[3])
    for copy in pending:
        copy.wait_send()


def shards(currents, radiate, receive, transfer_table, near_blocks, dir_offsets, trans_src, trans_tid, near_src):
    any_spec = pl.BlockSpec(memory_space=pl.ANY)
    dma = pltpu.SemaphoreType.DMA
    out = pl.pallas_call(
        body,
        out_shape=jax.ShapeDtypeStruct((6, 128, 256), BF),
        in_specs=[any_spec] * 9,
        out_specs=any_spec,
        scratch_shapes=[
            pltpu.VMEM((385, 128, 128), BF),
            pltpu.VMEM((12, 27, 128, 128), BF),
            pltpu.VMEM((TB, 192, 384), BF),
            pltpu.VMEM((TB, 384, 128), BF),
            pltpu.VMEM((192, TB, 128), BF),
            pltpu.VMEM((48, 4 * TB, 128), BF),
            pltpu.VMEM((2, 4, 18, 32, 128), BF),
            pltpu.VMEM((2, 3, 6, 32, 128), BF),
            pltpu.VMEM((2, 6, 128, 128), BF),
            pltpu.VMEM((3, 12, 128, 128), BF),
            pltpu.VMEM((2, 12, 128, 128), BF),
            pltpu.VMEM((12, 128, 128), F32),
            pltpu.VMEM((16, TB, 128), BF),
            pltpu.VMEM((16, TB, 384), BF),
            pltpu.VMEM((32, 144, 128), BF),
            pltpu.VMEM((TB, 128), BF),
            pltpu.VMEM((128, 384), BF),
            pltpu.VMEM((128, 384), BF),
            pltpu.VMEM((2, 6, 128, 128), BF),
            pltpu.VMEM((2, 6, 1, 27), jnp.int32),
            pltpu.VMEM((2, 6, 1, 27), jnp.int32),
            pltpu.SMEM((2, 6, 1, 27), jnp.int32),
            pltpu.VMEM((316, 384), BF),
            pltpu.VMEM((384, 384), F32),
            pltpu.VMEM((384, 384), BF),
            pltpu.VMEM((2, 48, 192), jnp.int32),
            pltpu.VMEM((128, 256), F32),
            pltpu.VMEM((256, 128), F32),
            pltpu.VMEM((256, 128), F32),
            pltpu.SMEM((33,), jnp.int32),
            dma((18,)),
            dma((4,)),
            dma((4,)),
            dma((48,)),
            dma((48,)),
            dma((17,)),
            dma((17,)),
            dma((42,)),
            dma((42,)),
            dma((6,)),
            dma((6,)),
        ],
        compiler_params=pltpu.CompilerParams(
            collective_id=0, has_side_effects=True, vmem_limit_bytes=67043328
        ),
        name="fmm",
    )(
        currents[0], radiate, receive, near_blocks[0], jnp.swapaxes(near_src, 0, 1), transfer_table,
        jnp.swapaxes(trans_src[0], 0, 1), jnp.swapaxes(trans_tid[0], 0, 1), dir_offsets,
    )
    return out[None]


def solution(mesh):
    placed = (
        P("region", "dir", None, None),
        P(),
        P(),
        P(),
        P("region", "dir", None, None, None),
        P(),
        P("region", None, None),
        P("region", None, None),
        P("region", "dir", None),
    )
    return jax.shard_map(
        shards,
        mesh=mesh,
        in_specs=placed,
        out_specs=P("region", "dir", None, None),
        check_vma=False,
    )
```

```python
import jax
import jax.numpy as jnp
from jax import lax
from jax.experimental import pallas as pl
from jax.experimental.pallas import tpu as pltpu
from jax.sharding import PartitionSpec as P

MESH = pl.DeviceIdType.MESH
BF = jnp.bfloat16
F32 = jnp.float32
TB = 96
CHUNKS = ((0, 0, 16), (0, 16, 32), (0, 48, 32), (0, 80, 16), (1, 0, 32), (1, 32, 32), (1, 64, 32))
RIM = 6
BLK = 12 + RIM
HALF = (BLK + 1) // 2


def m4(v):
    return lax.rem(v + 8, 4)


def body(
    cur_in, rad_in, rcv_in, nb_in, near_in, tt_in, src_in, tid_in, offs_in, out,
    cur, nb, mat, pat, tx, rx, relay, relay2, hop, ps, pr, acc, bpat, bmat, btr, rad, rcv, rw, fin,
    near_v, near_m, ns, tts, wide, tt_t, sraw, stage, src, tid, offs,
    lsem, psend, precv, asend, arecv, zsend, zrecv, rsend, rrecv, ssend, srecv,
):
    d = lax.axis_index("dir")
    z = lax.axis_index("region")
    c = lax.rem(d, 2)
    chip = lax.div(d, 2)
    x = lax.rem(chip, 4)
    y = lax.div(chip, 4)
    pa = x + c * (y - x)
    pb = y + c * (x - y)
    oc = 1 - c

    def dev(a, b, zz=None):
        xx = a + c * (b - a)
        yy = b + c * (a - b)
        return ((yy * 4 + xx) * 2 + c, z if zz is None else zz)

    partner = (d + 1 - 2 * c, z)
    a_up, a_dn = dev(m4(pa + 1), pb), dev(m4(pa - 1), pb)
    b_up, b_dn = dev(pa, m4(pb + 1)), dev(pa, m4(pb - 1))
    z_up, z_dn = dev(pa, pb, m4(z + 1)), dev(pa, pb, m4(z - 1))

    barrier = pltpu.get_barrier_semaphore()
    for peer in (z_up, z_dn, a_up, a_dn, b_up, b_dn, partner):
        pl.semaphore_signal(barrier, inc=1, device_id=peer, device_id_type=MESH)

    lane0 = pl.multiple_of(c * 128, 128)
    own_half = cur_in.at[:, :, pl.ds(lane0, 128)]

    def base(oa, ob):
        return (m4(pa - oa) * 4 + m4(pb - ob)) * BLK

    own0 = base(0, 0)
    loads = {}

    def load(name, src_ref, dst_ref):
        loads[name] = pltpu.make_async_copy(src_ref, dst_ref, lsem.at[len(loads)])
        loads[name].start()

    load("keep", own_half, cur.at[pl.ds(own0, 6)])
    load("src", src_in, sraw.at[0])
    load("tid", tid_in, sraw.at[1])
    load("tt", tt_in.at[:, pl.ds(pl.multiple_of(pb * 384, 128), 384)], tts)
    load("rad", rad_in.at[pl.ds(pl.multiple_of((pb * 4 + pa) * TB, 16), TB)], rad)
    load("rcv", rcv_in.at[:, pl.ds(pl.multiple_of(pb * 384, 128), 384)], rcv)
    load("near", near_in, near_v.at[0])
    load("offs", offs_in, offs)

    pl.semaphore_wait(barrier, 7)
    pending = []

    def remote(src_ref, dst_ref, send, recv, to):
        return pltpu.make_async_remote_copy(
            src_ref=src_ref, dst_ref=dst_ref, send_sem=send, recv_sem=recv,
            device_id=to, device_id_type=MESH,
        )

    def go(copy):
        copy.start()
        pending.append(copy)

    def arrived(ref, sem):
        remote(ref, ref, psend.at[0], sem, partner).wait_recv()

    count = [0]

    def send_main(oa, ob, lo, n, to, ra, rb, piece, origin=None):
        part = cur.at[pl.ds(base(oa, ob) + lo, n)]
        go(remote(part if origin is None else origin, part,
                  asend.at[count[0]], arecv.at[(ra * 4 + rb) * 3 + piece], to))
        count[0] += 1

    def got_main(oa, ob, lo, n, piece):
        arrived(cur.at[pl.ds(base(oa, ob) + lo, n)], arecv.at[(oa * 4 + ob) * 3 + piece])

    def z_target(oa, ob):
        a_, b_ = m4(pa - oa), m4(pb - ob)
        yb = b_ + c * (a_ - b_)
        return dev(pa, pb, m4(z + 2 * lax.div(yb, 2) - 1))

    def zb_at(oa, ob):
        a_, b_ = m4(pa - oa), m4(pb - ob)
        return 16 * BLK + ((a_ * 2 + lax.rem(b_, 2)) * 2 + lax.div(b_, 2)) * (12 - RIM)

    def send_zb(oa, ob):
        go(remote(
            cur.at[pl.ds(base(oa, ob) + RIM, 12 - RIM)], cur.at[pl.ds(zb_at(oa, ob), 12 - RIM)],
            zsend.at[oa * 4 + ob], zrecv.at[oa * 4 + ob], z_target(oa, ob),
        ))

    def got_zb(oa, ob):
        arrived(cur.at[pl.ds(zb_at(oa, ob), 12 - RIM)], zrecv.at[oa * 4 + ob])

    def send_own(lo, n, piece, origin=None):
        send_main(0, 0, lo, n, a_up, 1, 0, piece, origin)
        send_main(0, 0, lo, n, a_dn, 3, 0, piece, origin)
        send_main(0, 0, lo, n, b_up, 0, 1, piece, origin)
        send_main(0, 0, lo, n, b_dn, 0, 3, piece, origin)

    go(remote(
        cur_in.at[:, :, pl.ds(pl.multiple_of(oc * 128, 128), 128)],
        cur.at[pl.ds((pb * 4 + pa) * BLK + 6, 6)], psend.at[0], precv.at[0], partner,
    ))
    go(remote(
        cur_in.at[pl.ds(0, RIM), :, pl.ds(lane0, 128)], cur.at[pl.ds(own0 + 12, RIM)],
        zsend.at[16], zrecv.at[16], z_target(0, 0),
    ))
    send_own(0, 6, 0, own_half)
    go(remote(near_in, near_v.at[1], psend.at[1], precv.at[1], partner))
    loads["keep"].wait()
    arrived(cur.at[pl.ds(own0 + 6, 6)], precv.at[0])
    send_own(6, 6, 1)
    send_zb(0, 0)
    arrived(cur.at[pl.ds(own0 + 12, RIM)], zrecv.at[16])
    send_own(12, RIM, 2)
    load("nb", nb_in, nb.at[pl.ds(0, 6)])
    go(remote(nb_in, nb.at[pl.ds(6, 6)], psend.at[2], precv.at[2], partner))
    cur[384] = jnp.zeros((128, 128), BF)

    def slot_of(s, field):
        halo = (s < 96) | (s >= 288)
        i = jnp.where(s < 96, s + 96, jnp.where(s >= 288, s - 288, s - 96))
        box_chip = lax.shift_right_arithmetic(i * 5462, 16)
        p = i - 12 * box_chip - 6 * c
        p = jnp.where(p < 0, p + 12, p)
        by = lax.shift_right_arithmetic(box_chip, 2)
        bx = box_chip - 4 * by
        a = bx + c * (by - bx)
        b = by + c * (bx - by)
        b_hi = lax.shift_right_arithmetic(b, 1)
        size, rim = (BLK, RIM) if field else (16, 4)
        main = (a * 4 + b) * size + p
        beyond = 16 * size + ((a * 2 + b - 2 * b_hi) * 2 + b_hi) * (12 - rim) + (p - rim)
        slot = jnp.where(halo, jnp.where(p < rim, main + 12, beyond), main)
        low = jnp.where(z == 0, 96, 0)
        high = jnp.where(z == 3, 288, 384)
        return jnp.where((s < low) | (s >= high), -1, slot)

    def table(values, ref):
        stage[...] = jnp.full((128, 256), -1.0, F32)
        stage[0:48, 0:192] = values
        stage[64:112, 0:192] = values
        ref[0:128, :] = jnp.transpose(stage[:, 0:128])
        ref[128:256, :] = jnp.transpose(stage[:, 128:256])

    def pattern_block(at, box):
        for i in range(8):
            two = jnp.concatenate([cur[box(2 * i)], cur[box(2 * i + 1)]], axis=1)
            o = jnp.dot(rad[...], two, preferred_element_type=F32)
            bpat[2 * i] = o[:, :128].astype(BF)
            bpat[2 * i + 1] = o[:, 128:].astype(BF)

        def turn(i, _):
            t0 = pl.multiple_of(i * 16, 16)
            pat[pl.ds(t0, 16), pl.ds(at, 16), :] = jnp.swapaxes(bpat[:, pl.ds(t0, 16), :], 0, 1)
            return 0

        lax.fori_loop(0, TB // 16, turn, 0, unroll=2)

    def patterns(*blocks):
        for oa, ob in blocks:
            first = base(oa, ob)
            at = (m4(pa - oa) * 4 + m4(pb - ob)) * 16
            pattern_block(pl.multiple_of(at, 16), lambda i, first=first: first + i)

    def pattern_zb(oa, ob):
        got_zb(oa, ob)
        got_zb(oa, ob + 2)
        a_, parity = m4(pa - oa), lax.rem(m4(pb - ob), 2)
        g = a_ * 2 + parity
        rim0 = (a_ * 4 + parity) * BLK + 16
        over0 = 16 * BLK + g * 2 * (12 - RIM)

        def box(i):
            second, q = i // 8, i % 8
            return rim0 + second * 2 * BLK + q if q < RIM - 4 else over0 + second * (12 - RIM) + q - (RIM - 4)

        pattern_block(pl.multiple_of(256 + g * 16, 16), box)

    n_iota = lax.broadcasted_iota(jnp.int32, (384, 128), 0).astype(F32)
    lane = lax.broadcasted_iota(jnp.int32, (TB, 128), 1)

    def box_row(jp):
        late = jnp.where(jp >= 144, 1, 0)
        at = jp - 144 * late
        size = 36 - 24 * late
        a_ = lax.div(at * (1 + 2 * late), 36)
        rest = at - a_ * size
        which = lax.div(rest, 12)
        p = rest - which * 12
        b_ = m4(pb + jnp.where(late == 1, 0, jnp.where(which == 2, 3, 2 - which)))
        chip_ = (b_ + c * (a_ - b_)) * 4 + a_ + c * (b_ - a_)
        return chip_ * 12 + lax.rem(p + 6 * c, 12)

    def hot(ref, lo, hi):
        row = jnp.where(lane[:1] < 64, ref[pl.ds(lo, 1), :], ref[pl.ds(hi, 1), :])
        return jnp.where(n_iota == row, 1.0, 0.0).astype(BF)

    def mat_group(g):
        def two_rows(it, _):
            rows = [(box_row(g * 16 + 2 * it + p), box_row(g * 16 + 8 + 2 * it + p)) for p in range(2)]
            classes = jnp.concatenate([hot(tid, *rows[0]), hot(tid, *rows[1])], axis=1)
            coef = jnp.dot(
                tt_t[pl.ds(pl.multiple_of(pa * TB, 16), TB), :], classes, preferred_element_type=F32
            )
            for p in range(2):
                part = coef[:, p * 128 : (p + 1) * 128]
                both = jnp.concatenate(
                    [jnp.where(lane < 64, part, 0.0), jnp.where(lane < 64, 0.0, part)], axis=0
                ).astype(BF)
                placed = lax.dot_general(
                    both, hot(src, *rows[p]), (((1,), (1,)), ((), ())), preferred_element_type=F32
                )
                for h in range(2):
                    bmat[h * 8 + 2 * it + p] = placed[h * TB : (h + 1) * TB].astype(BF)
            return 0

        lax.fori_loop(0, 4, two_rows, 0, unroll=4)
        j0 = pl.multiple_of(g * 16, 16)

        def turn(i, _):
            t0 = pl.multiple_of(i * 16, 16)
            for q in range(3):
                lanes = slice(q * 128, (q + 1) * 128)
                mat[pl.ds(t0, 16), pl.ds(j0, 16), lanes] = jnp.swapaxes(bmat[:, pl.ds(t0, 16), lanes], 0, 1)
            return 0

        lax.fori_loop(0, TB // 16, turn, 0)

    def mats(lo, hi):
        lax.fori_loop(lo, hi, lambda g, _: (mat_group(g), 0)[1], 0)

    def line_event(oa):
        send_main(oa, 0, 0, BLK, b_up, oa, 1, 0)
        send_main(oa, 0, 0, BLK, b_dn, oa, 3, 0)

    odd = lax.rem(y, 2)
    line1 = 3 - 2 * c * (1 - odd)
    line2 = 1 + c
    line3 = 2 + c * (1 - 2 * odd)

    def halves(oa, ob):
        got_main(oa, ob, 0, HALF, 0)
        got_main(oa, ob, HALF, BLK - HALF, 1)
        send_zb(oa, ob)

    def ring_event(oa):
        for ob, lo, n, to, piece in ((1, 0, HALF, b_up, 0), (3, HALF, BLK - HALF, b_dn, 1)):
            got_main(oa, ob, 0, BLK, 0)
            send_main(oa, ob, lo, n, to, oa, 2, piece)
            send_zb(oa, ob)

    for oa, ob in ((1, 0), (3, 0), (0, 1), (0, 3)):
        got_main(oa, ob, 0, 6, 0)
        got_main(oa, ob, 6, 6, 1)
        if (oa, ob) == (1, 0):
            send_main(1, 0, 0, HALF, a_up, 2, 0, 0)
        if (oa, ob) == (0, 1):
            send_main(0, 1, 0, HALF, b_up, 0, 2, 0)
        send_zb(oa, ob)
    got_main(3, 0, 12, RIM, 2)
    send_main(3, 0, HALF, BLK - HALF, a_dn, 2, 0, 1)
    got_main(1, 0, 12, RIM, 2)
    line_event(line1)
    got_main(0, 3, 12, RIM, 2)
    send_main(0, 3, HALF, BLK - HALF, b_dn, 0, 2, 1)
    got_main(0, 1, 12, RIM, 2)
    loads["src"].wait()
    table(slot_of(sraw[0], False).astype(F32), src)
    loads["tid"].wait()
    table(sraw[1].astype(F32), tid)
    loads["tt"].wait()
    wide[...] = jnp.zeros((384, 384), F32)
    wide[0:316, :] = tts[...].astype(F32)
    tt_t[...] = jnp.transpose(wide[...]).astype(BF)
    loads["rad"].wait()
    halves(2, 0)
    line_event(line2)
    mats(0, 1)
    patterns((0, 0))
    mats(1, 2)
    patterns((1, 0))
    ring_event(line1)
    line_event(line3)
    mats(2, 3)
    patterns((3, 0), (2, 0))
    halves(0, 2)
    mats(3, 5)
    patterns((0, 1), (0, 3))
    ring_event(line2)
    mats(5, 7)
    patterns((line1, 1), (line1, 3), (0, 2))
    halves(line1, 2)
    mats(7, 9)
    patterns((line2, 1), (line2, 3))
    ring_event(line3)
    mats(9, 12)
    halves(line2, 2)
    patterns((line3, 1), (line3, 3), (line1, 2), (line2, 2))
    halves(line3, 2)
    patterns((line3, 2))
    for oa, ob in (
        (0, 0), (0, 1), (line1, 1), (line1, 0), (line2, 1), (line2, 0), (line3, 1), (line3, 0)
    ):
        pattern_zb(oa, ob)

    first_row, rows_of = (0, 144), (36, 12)
    own_copies = []

    def chunk(n):
        h, t_first, n_dirs = CHUNKS[n]
        j0, n_rows = first_row[h], rows_of[h]
        n_half, n_tiles = n_rows // 2, n_rows // 4

        def one(i, _):
            t = t_first + i
            o = jnp.dot(mat[t, j0 : j0 + 4 * n_rows, :], pat[t], preferred_element_type=F32)
            btr[i, 0 : 4 * n_rows] = o.astype(BF)
            return 0

        lax.fori_loop(0, n_dirs, one, 0, unroll=8)

        def pack(i, _):
            r0 = pl.multiple_of(lax.rem(i, n_tiles) * 16, 16)
            t0 = pl.multiple_of(lax.div(i, n_tiles) * 16, 16)
            tx[pl.ds(j0 + r0, 16), pl.ds(t_first + t0, 16), :] = jnp.swapaxes(
                btr[pl.ds(t0, 16), pl.ds(r0, 16), :], 0, 1
            )
            return 0

        lax.fori_loop(0, n_tiles * n_dirs // 16, pack, 0, unroll=3)
        ts = pl.ds(t_first, n_dirs)
        here = pl.ds(h * 36, n_rows)
        there = rx_at(pa, n)
        far = j0 + m4(pa + 2) * n_rows
        for way, to in ((0, a_up), (1, a_dn)):
            go(remote(tx.at[pl.ds(far + way * n_half, n_half), ts], held(way, n),
                      rsend.at[n * 6 + 2 + way], rrecv.at[n * 6 + 2 + way], to))
        for way, o, to in ((0, 1, a_up), (1, -1, a_dn)):
            go(remote(tx.at[pl.ds(j0 + m4(pa + o) * n_rows, n_rows), ts], rx.at[here, there],
                      rsend.at[n * 6 + way], rrecv.at[n * 6 + way], to))
        own = pltpu.make_async_copy(tx.at[pl.ds(j0 + pa * n_rows, n_rows), ts], rx.at[here, there], lsem.at[10 + n])
        own.start()
        own_copies.append(own)

    def rx_at(a_, n):
        _, t_first, n_dirs = CHUNKS[n]
        return pl.ds(pl.multiple_of(a_ * TB + t_first, 16), n_dirs)

    def held(way, n):
        h, _, n_dirs = CHUNKS[n]
        return relay.at[way, n, :, pl.ds(0, n_dirs)] if h == 0 else relay2.at[way, n - 4]

    def forward(n):
        h = CHUNKS[n][0]
        n_half = rows_of[h] // 2
        for way, o, to in ((0, -1, a_up), (1, 1, a_dn)):
            arrived(held(way, n), rrecv.at[n * 6 + 2 + way])
            go(remote(held(way, n), rx.at[pl.ds(h * 36 + way * n_half, n_half), rx_at(m4(pa + o), n)],
                      rsend.at[n * 6 + 4 + way], rrecv.at[n * 6 + 4 + way], to))

    def all_here(h):
        n_half = rows_of[h] // 2
        here = pl.ds(h * 36, 2 * n_half)
        for n in range(len(CHUNKS)):
            if CHUNKS[n][0] != h:
                continue
            own_copies[n].wait()
            arrived(rx.at[here, rx_at(m4(pa - 1), n)], rrecv.at[n * 6])
            arrived(rx.at[here, rx_at(m4(pa + 1), n)], rrecv.at[n * 6 + 1])
            for way in range(2):
                arrived(rx.at[pl.ds(h * 36 + way * n_half, n_half), rx_at(m4(pa + 2), n)],
                        rrecv.at[n * 6 + 4 + way])

    def near_boxes(which, lo, hi):
        def box(i, _):
            w = which * 6 + i
            total = jnp.zeros((128, 128), F32)
            for m in range(0, 26, 2):
                blocks = jnp.concatenate([nb[w, m], nb[w, m + 1]], axis=1)
                fields = jnp.concatenate([cur[ns[which, i, 0, m]], cur[ns[which, i, 0, m + 1]]], axis=0)
                total += jnp.dot(blocks, fields, preferred_element_type=F32)
            total += jnp.dot(nb[w, 26], cur[ns[which, i, 0, 26]], preferred_element_type=F32)
            acc[w] = total
            return 0

        lax.fori_loop(lo, hi, box, 0)

    def contract(group, put):
        def pair(i, _):
            j = group * 12 + 2 * i
            two = jnp.concatenate([rx[j], rx[j + 1]], axis=1)
            o = jnp.dot(rw[...], two, preferred_element_type=F32)
            put(2 * i, o[:, :128])
            put(2 * i + 1, o[:, 128:])
            return 0

        lax.fori_loop(0, 6, pair, 0)

    def put_acc(w, v):
        acc[w] = acc[w] + v

    chunk(0)
    chunk(1)
    forward(0)
    chunk(2)
    loads["rcv"].wait()
    loads["offs"].wait()
    k_at = lax.broadcasted_iota(jnp.int32, (8, 384), 1) + pb * 384
    width = jnp.zeros((8, 384), jnp.int32)
    for i in range(32):
        lo, hi = offs[i], offs[i + 1]
        width = jnp.where((k_at >= lo) & (k_at < hi), hi - lo, width)
    weight = 1536.0 / (32.0 * width.astype(F32))
    rw[...] = (rcv[...].astype(F32) * weight[:1]).astype(BF)
    loads["near"].wait()
    arrived(near_v.at[1], precv.at[1])
    near_s = near_v[...]
    near_s = slot_of(jnp.where(near_s < 0, -1, near_s + 48), True)
    near_m[...] = jnp.where(near_s < 0, 384, near_s)
    forward(1)
    load("ns", near_m, ns)
    chunk(3)
    chunk(4)
    forward(2)
    chunk(5)
    chunk(6)
    loads["ns"].wait()
    loads["nb"].wait()
    near_boxes(0, 0, 1)
    forward(3)
    near_boxes(0, 1, 4)
    forward(4)
    all_here(0)

    def put_ps(slot):
        def put(w, v):
            ps[slot, w] = v.astype(BF)

        return put

    contract(0, put_ps(2))
    go(remote(ps.at[2, pl.ds(0, 6)], hop.at[0], ssend.at[0], srecv.at[0], b_up))
    go(remote(ps.at[2, pl.ds(6, 6)], hop.at[1], ssend.at[1], srecv.at[1], b_dn))
    contract(1, put_ps(0))
    go(remote(ps.at[0, pl.ds(6, 6)], pr.at[0, pl.ds(6, 6)], ssend.at[2], srecv.at[2], b_up))
    contract(2, put_ps(1))
    go(remote(ps.at[1, pl.ds(0, 6)], pr.at[1, pl.ds(0, 6)], ssend.at[3], srecv.at[3], b_dn))
    forward(5)
    forward(6)
    near_boxes(0, 4, 6)
    for way, to in ((0, b_up), (1, b_dn)):
        arrived(hop.at[way], srecv.at[way])

        def join(i, _, way=way):
            w = way * 6 + i
            ps[way, w] = (ps[way, w].astype(F32) + hop[way, i].astype(F32)).astype(BF)
            return 0

        lax.fori_loop(0, 6, join, 0)
        part = pl.ds(way * 6, 6)
        go(remote(ps.at[way, part], pr.at[way, part], ssend.at[4 + way], srecv.at[4 + way], to))
    arrived(nb.at[pl.ds(6, 6)], precv.at[2])
    near_boxes(1, 0, 6)
    all_here(1)
    contract(3, put_acc)
    arrived(pr.at[0, pl.ds(6, 6)], srecv.at[2])
    arrived(pr.at[1, pl.ds(0, 6)], srecv.at[3])
    arrived(pr.at[0, pl.ds(0, 6)], srecv.at[4])
    arrived(pr.at[1, pl.ds(6, 6)], srecv.at[5])

    def finish(which):
        def one(i, _):
            w = which * 6 + i
            total = acc[w] + pr[0, w].astype(F32) + pr[1, w].astype(F32)
            fin[which, i] = total.astype(BF)
            return 0

        lax.fori_loop(0, 6, one, 0)

    mine = pl.ds(lane0, 128)
    theirs = pl.ds(pl.multiple_of(oc * 128, 128), 128)
    finish(1)
    go(remote(fin.at[1], out.at[:, :, mine], psend.at[3], precv.at[3], partner))
    finish(0)
    write = pltpu.make_async_copy(fin.at[0], out.at[:, :, mine], lsem.at[17])
    write.start()
    write.wait()
    arrived(out.at[:, :, theirs], precv.at[3])
    for copy in pending:
        copy.wait_send()


def shards(currents, radiate, receive, transfer_table, near_blocks, dir_offsets, trans_src, trans_tid, near_src):
    any_spec = pl.BlockSpec(memory_space=pl.ANY)
    dma = pltpu.SemaphoreType.DMA
    out = pl.pallas_call(
        body,
        out_shape=jax.ShapeDtypeStruct((6, 128, 256), BF),
        in_specs=[any_spec] * 9,
        out_specs=any_spec,
        scratch_shapes=[
            pltpu.VMEM((385, 128, 128), BF),
            pltpu.VMEM((12, 27, 128, 128), BF),
            pltpu.VMEM((TB, 192, 384), BF),
            pltpu.VMEM((TB, 384, 128), BF),
            pltpu.VMEM((192, TB, 128), BF),
            pltpu.VMEM((48, 4 * TB, 128), BF),
            pltpu.VMEM((2, 4, 18, 32, 128), BF),
            pltpu.VMEM((2, 3, 6, 32, 128), BF),
            pltpu.VMEM((2, 6, 128, 128), BF),
            pltpu.VMEM((3, 12, 128, 128), BF),
            pltpu.VMEM((2, 12, 128, 128), BF),
            pltpu.VMEM((12, 128, 128), F32),
            pltpu.VMEM((16, TB, 128), BF),
            pltpu.VMEM((16, TB, 384), BF),
            pltpu.VMEM((32, 144, 128), BF),
            pltpu.VMEM((TB, 128), BF),
            pltpu.VMEM((128, 384), BF),
            pltpu.VMEM((128, 384), BF),
            pltpu.VMEM((2, 6, 128, 128), BF),
            pltpu.VMEM((2, 6, 1, 27), jnp.int32),
            pltpu.VMEM((2, 6, 1, 27), jnp.int32),
            pltpu.SMEM((2, 6, 1, 27), jnp.int32),
            pltpu.VMEM((316, 384), BF),
            pltpu.VMEM((384, 384), F32),
            pltpu.VMEM((384, 384), BF),
            pltpu.VMEM((2, 48, 192), jnp.int32),
            pltpu.VMEM((128, 256), F32),
            pltpu.VMEM((256, 128), F32),
            pltpu.VMEM((256, 128), F32),
            pltpu.SMEM((33,), jnp.int32),
            dma((18,)),
            dma((4,)),
            dma((4,)),
            dma((48,)),
            dma((48,)),
            dma((17,)),
            dma((17,)),
            dma((42,)),
            dma((42,)),
            dma((6,)),
            dma((6,)),
        ],
        compiler_params=pltpu.CompilerParams(
            collective_id=0, has_side_effects=True, vmem_limit_bytes=67043328
        ),
        name="fmm",
    )(
        currents[0], radiate, receive, near_blocks[0], jnp.swapaxes(near_src, 0, 1), transfer_table,
        jnp.swapaxes(trans_src[0], 0, 1), jnp.swapaxes(trans_tid[0], 0, 1), dir_offsets,
    )
    return out[None]


def solution(mesh):
    placed = (
        P("region", "dir", None, None),
        P(),
        P(),
        P(),
        P("region", "dir", None, None, None),
        P(),
        P("region", None, None),
        P("region", None, None),
        P("region", "dir", None),
    )
    return jax.shard_map(
        shards,
        mesh=mesh,
        in_specs=placed,
        out_specs=P("region", "dir", None, None),
        check_vma=False,
    )
```
